128 devices in a mesh: ctx: 32 (over x, z, core), grp: 4 (over y).
Axes of the slice: x: 4, y: 4, z: 4, core: 2. Of those that a mesh axis runs over, the one named last changes fastest.
Arguments:
- query_heads: bfloat16 [16384, 2048], P('ctx', 'grp'), may hold values from -6 to 6
- key_heads: bfloat16 [16384, 2048], P('ctx', 'grp'), may hold values from -6 to 6
- value_heads: bfloat16 [16384, 2048], P('ctx', 'grp'), may hold values from -6 to 6
- log_decay: float32 [16, 16384], P('grp', 'ctx'), may hold values from -1 to 0
- residual: bfloat16 [16384, 2048], P(('ctx', 'grp')), may hold values from -4 to 4
- out_weight: bfloat16 [2048, 2048], replicated, may hold values from -0.5 to 0.5
- norm_gain: float32 [2048], replicated, may hold values from 0.25 to 1.75
- expert_ids: int32 [16384, 6], P(('ctx', 'grp')), may hold values from 0 to 63, all different within a row; in each aligned block of 128 rows (0 to 127, 128 to 255, ...) at most 15 rows name the same one
- gate_weights: float32 [16384, 6], P(('ctx', 'grp')), may hold values from 0.1 to 1
- gate_proj: bfloat16 [64, 2048, 1408], P('ctx', None, 'grp'), may hold values from -0.125 to 0.125
- up_proj: bfloat16 [64, 2048, 1408], P('ctx', None, 'grp'), may hold values from -0.125 to 0.125
- down_proj: bfloat16 [64, 1408, 2048], P('ctx', 'grp'), may hold values from -0.15625 to 0.15625
Outputs:
- attended: bfloat16 [16384, 2048], P(('ctx', 'grp'))
- layer_out: bfloat16 [16384, 2048], P(('ctx', 'grp'))
The draws below stay inside these ranges and needn't reach their ends.
Inputs may be any that keep to these rules, and one draw needn't show every extreme that they name: `expert_ids`: each token names 6 different experts. In each aligned block of 128 tokens no expert is named by more than 15 tokens, and that bound is reached.
All inputs are finite; a program needn't handle non-finite values.
Results may differ from the reference program's by a relative error of at most 0.02.
Values may be sent and summed in bfloat16 or wider, within the bound.
No kernel may reach another device: no remote copies, remote signals or barrier semaphores. Data moves between devices by JAX's collectives and lax.ppermute only.
A program may use at most 128 MiB of HBM per device.

```python
import math
import jax
import jax.numpy as jnp
import numpy as np
from jax import lax

D = 2048
HEAD_COUNT = 16
HD = 128
E = 64
FF = 1408
TOPK = 6
TOK_DEV = 512
TOKENS = 16384
ROWS = 128
CAP = 15
N_GRP = 4


def draw_log_decay(key, part):
    random_subkeys = jax.random.split(jax.random.fold_in(key, 17), 7)
    ordering = jax.random.permutation(random_subkeys[0], HEAD_COUNT)
    slow_count = HEAD_COUNT // 2
    slow_head = ordering < slow_count
    slow_rate = jnp.exp(jax.random.uniform(random_subkeys[1], (HEAD_COUNT,), jnp.float32, math.log(0.05 / TOKENS), math.log(0.3 / TOKENS)))
    fast_rate = jnp.exp(jax.random.uniform(random_subkeys[2], (HEAD_COUNT,), jnp.float32, math.log(0.02), math.log(0.1)))
    decay_rate = jnp.where(slow_head, slow_rate, fast_rate)
    segments = TOKENS // TOK_DEV
    segment_factor = jnp.exp(jax.random.uniform(random_subkeys[3], (HEAD_COUNT, segments), jnp.float32, math.log(0.5), math.log(2.0)))
    jitter = jax.random.uniform(random_subkeys[4], (HEAD_COUNT, TOKENS), jnp.float32, 0.5, 1.5)
    decay_floor = -decay_rate[:, None] * jnp.repeat(segment_factor, TOK_DEV, axis=1) * jitter
    widening_factor = TOKENS // 3
    spike_position = jnp.arange(3, dtype=jnp.int32) * widening_factor + jax.random.randint(random_subkeys[5], (3,), 0, widening_factor)
    spike_retain = jax.random.uniform(random_subkeys[6], (HEAD_COUNT, 3), jnp.float32, 0.5, 0.8)
    token_positions = jnp.arange(TOKENS, dtype=jnp.int32)
    spike_matches = (token_positions[None, :] == spike_position[:, None]).astype(jnp.float32)
    decay_floor = decay_floor + jnp.dot(jnp.log(spike_retain), spike_matches)
    return decay_floor.astype(jnp.float32)


def block_scale(rng, extent, shards, low, largest):
    loudness, own = 1.0, jax.random.fold_in(rng, 6)
    for axis_at, parts in shards:
        draws = jnp.exp(jax.random.uniform(jax.random.fold_in(own, axis_at), (parts,), jnp.float32, low / len(shards), largest / len(shards)))
        loudness = loudness * jnp.repeat(draws, extent[axis_at] // parts).reshape([-1 if axis == axis_at else 1 for axis in range(len(extent))])
    return loudness


def assign_block(rng, own, number, rows, amount, top, limit, lean):
    order = jax.random.permutation(rng, amount)
    heavy_load, ordinary = portions_of(amount, rows * top, limit, lean, True), portions_of(amount, rows * top, limit, lean, False)
    places = jnp.arange(amount)

    def named(lengths, offset_by):
        used = int((lengths > 0).sum())
        fixed = max(1, used // 4)
        shifted = fixed + (places - fixed + offset_by * (used - fixed)) % max(1, amount - fixed)
        return jnp.zeros((amount,), jnp.int32).at[order[jnp.where(places < fixed, places, shifted)]].set(jnp.asarray(lengths, jnp.int32))

    lengths = jnp.where(number % 4 == 0, named(heavy_load, number // 4), named(ordinary, number - number // 4 - 1))
    mixed = jax.random.permutation(jax.random.fold_in(own, 3), amount)
    giver, sink = mixed[0:amount // 2 * 2:2], mixed[1:amount // 2 * 2:2]
    room = jnp.minimum(lengths[giver] - 1, limit - lengths[sink]) // 2
    room = jnp.where((giver == order[0]) | (sink == order[0]) | (lengths[sink] == 0), 0, jnp.maximum(room, 0))
    shifted = jax.random.randint(jax.random.fold_in(own, 4), (amount // 2,), 0, 1 << 20) % (room + 1)
    lengths = lengths.at[giver].add(-shifted).at[sink].add(shifted)
    members = jnp.searchsorted(jnp.cumsum(lengths), jnp.arange(rows * top), side="right").astype(jnp.int32)
    table = members.reshape(top, rows).T
    table = table[jax.random.permutation(jax.random.fold_in(own, 1), rows)]
    offset_by = jax.random.randint(jax.random.fold_in(own, 2), (rows, 1), 0, top)
    return jnp.take_along_axis(table, (jnp.arange(top)[None, :] + offset_by) % top, axis=1)


def portions_of(number_of, total, most, skew, full):
    portions = [(1 << 20) // math.isqrt(grade ** skew) + 1 for grade in range(1, number_of + 1)]
    largest = most if full else min(most, max(-(-total // number_of), total * portions[0] // sum(portions)))
    least = 1 if total - largest >= number_of - 1 else 0
    holding, rest = [largest] + [least] * (number_of - 1), total - largest - least * (number_of - 1)
    while rest > 0:
        candidates = [i for i in range(1, number_of) if holding[i] < largest] or [i for i in range(1, number_of) if holding[i] < most]
        mass, budget = sum([portions[i] for i in candidates]), rest
        for i in candidates:
            more = min(most - holding[i], max(1, budget * portions[i] // mass), rest)
            holding[i] = holding[i] + more
            rest = rest - more
    return np.array(holding)


def normal_values(rng, extent, scale, bound, cuts=(), held_as=jnp.bfloat16):
    drawn = scale * jax.random.normal(rng, extent, jnp.float32)
    if cuts:
        drawn = drawn * block_scale(rng, extent, cuts, -0.22, 0.18)
    return jnp.clip(drawn, -bound, bound).astype(held_as)


def setup_inputs(seed: int = 0) -> dict:
    streams_of = jax.random.split(jax.random.key(seed), 13)
    query_heads = normal_values(streams_of[0], (TOKENS, HEAD_COUNT * HD), 1.0, 6.0, ((0, 32), (1, 4)))
    key_heads = normal_values(streams_of[1], (TOKENS, HEAD_COUNT * HD), 1.0, 6.0, ((0, 32), (1, 4)))
    value_heads = normal_values(streams_of[2], (TOKENS, HEAD_COUNT * HD), 1.0, 6.0, ((0, 32), (1, 4)))
    log_decay = draw_log_decay(jax.random.fold_in(streams_of[12], 71), 0)
    residual = normal_values(streams_of[4], (TOKENS, D), 0.5, 4.0, ((0, 128),))
    out_weight = normal_values(streams_of[5], (HEAD_COUNT * HD, D), HD ** -0.5, 0.5)
    norm_gain = jnp.clip(1.0 + 0.15 * jax.random.normal(streams_of[6], (D,), jnp.float32), 0.25, 1.75)
    expert_ids_keys = jax.random.split(jax.random.fold_in(streams_of[7], 1), TOKENS // ROWS)
    expert_ids_turns = jax.random.permutation(jax.random.fold_in(streams_of[7], 3), TOKENS // ROWS)
    expert_ids = jax.vmap(lambda own, number: assign_block(jax.random.fold_in(streams_of[7], 2), own, number, ROWS, E, TOPK, CAP, 2))(expert_ids_keys, expert_ids_turns).reshape((TOKENS, TOPK))
    gate_weights = jnp.clip(0.1 + 0.9 * jax.random.uniform(streams_of[8], (TOKENS, TOPK), jnp.float32) ** block_scale(streams_of[8], (TOKENS, TOPK), ((0, 128),), -0.2, 0.2), 0.1, 1.0)
    gate_proj = normal_values(streams_of[9], (E, D, FF), D ** -0.5, 0.125, ((0, 32), (2, 4)))
    up_proj = normal_values(streams_of[10], (E, D, FF), D ** -0.5, 0.125, ((0, 32), (2, 4)))
    down_proj = normal_values(streams_of[11], (E, FF, D), FF ** -0.5, 0.15625, ((0, 32), (1, 4)))
    return {"query_heads": query_heads, "key_heads": key_heads, "value_heads": value_heads, "log_decay": log_decay, "residual": residual, "out_weight": out_weight, "norm_gain": norm_gain, "expert_ids": expert_ids, "gate_weights": gate_weights, "gate_proj": gate_proj, "up_proj": up_proj, "down_proj": down_proj}


def feature_map(values):
    return (jax.nn.elu(values.astype(jnp.float32)) + 1.0).astype(jnp.bfloat16)

def block_attention(feat_query, feat_key, value_rows, decay_rows, preceding_state, prior_norm):
    length = feat_query.shape[0]
    cumulative = jnp.cumsum(decay_rows, axis=1)
    block_total = cumulative[:, -1]
    query_wide = feat_query.astype(jnp.float32)
    key_wide = feat_key.astype(jnp.float32)
    value_broad = value_rows.astype(jnp.float32)
    scores = jnp.einsum('thd,shd->hts', query_wide, key_wide)
    row_index = lax.broadcasted_iota(jnp.int32, (length, length), 0)
    col_index = lax.broadcasted_iota(jnp.int32, (length, length), 1)
    causal = (col_index <= row_index)[None]
    spread = cumulative[:, :, None] - cumulative[:, None, :]
    weights = jnp.where(causal, scores * jnp.exp(jnp.where(causal, spread, 0.0)), 0.0)
    inner_den = lax.optimization_barrier(jnp.sum(weights, axis=2)).T
    inner_num = jnp.einsum('hts,shd->thd', weights.astype(jnp.bfloat16).astype(jnp.float32), value_broad)
    query_damping = query_wide * jnp.exp(cumulative).T[:, :, None]
    outer_numerator = jnp.einsum('cnm,nmp->cnp', query_damping, preceding_state, precision=lax.Precision.HIGHEST)
    outer_den = jnp.einsum('thk,hk->th', query_damping, prior_norm, precision=lax.Precision.HIGHEST)
    mixed_rows = ((inner_num + outer_numerator) / (inner_den + outer_den)[:, :, None]).astype(jnp.bfloat16)
    trailing_keys = key_wide * jnp.exp(block_total[:, None] - cumulative).T[:, :, None]
    shard_state = jnp.einsum('jfi,jfx->fix', trailing_keys.astype(jnp.bfloat16).astype(jnp.float32), value_broad)
    local_norm = lax.optimization_barrier(jnp.sum(trailing_keys, axis=0))
    return (mixed_rows.reshape(length, -1), block_total, shard_state, local_norm)

def route_block(block_ids, block_gates, block_normed):
    onehot = (block_ids[:, :, None] == jnp.arange(E, dtype=jnp.int32)).astype(jnp.int32)
    flat_hits = onehot.reshape(ROWS * TOPK, E)
    earlier = jnp.cumsum(flat_hits, axis=0) - flat_hits
    slot_index = lax.optimization_barrier(jnp.sum(earlier * flat_hits, axis=1)).reshape(ROWS, TOPK)
    target = block_ids * CAP + slot_index
    placed = (target[:, :, None] == jnp.arange(E * CAP, dtype=jnp.int32)).astype(jnp.float32)
    dispatch_rows = lax.optimization_barrier(jnp.sum(placed, axis=1)).astype(jnp.bfloat16)
    combiner = lax.optimization_barrier(jnp.sum(placed * block_gates.astype(jnp.bfloat16).astype(jnp.float32)[:, :, None], axis=1)).astype(jnp.bfloat16)
    buffer = jnp.dot(dispatch_rows.T, block_normed, preferred_element_type=jnp.float32).astype(jnp.bfloat16)
    return (buffer.reshape(E, CAP, D), combiner)

def reference(query_heads, key_heads, value_heads, log_decay, residual, out_weight, norm_gain, expert_ids, gate_weights, gate_proj, up_proj, down_proj):
    blocks = TOKENS // TOK_DEV
    feat_query = feature_map(query_heads).reshape(blocks, TOK_DEV, HEAD_COUNT, HD)
    feat_key = feature_map(key_heads).reshape(blocks, TOK_DEV, HEAD_COUNT, HD)
    value_rows = value_heads.reshape(blocks, TOK_DEV, HEAD_COUNT, HD)
    decay_rows = log_decay.reshape(HEAD_COUNT, blocks, TOK_DEV).transpose(1, 0, 2)

    def advance(running, packed):
        preceding_state, prior_norm = running
        mixed_rows, block_total, shard_state, local_norm = block_attention(packed[0], packed[1], packed[2], packed[3], preceding_state, prior_norm)
        factor = jnp.exp(block_total)
        return ((factor[:, None, None] * preceding_state + shard_state, factor[:, None] * prior_norm + local_norm), mixed_rows)
    start_state = (jnp.zeros((HEAD_COUNT, HD, HD), jnp.float32), jnp.zeros((HEAD_COUNT, HD), jnp.float32))
    _, head_rows = lax.scan(advance, start_state, (feat_query, feat_key, value_rows, decay_rows))
    head_rows = head_rows.reshape(TOKENS, HEAD_COUNT * HD)
    projected = jnp.dot(head_rows, out_weight, preferred_element_type=jnp.float32)
    attended = (residual.astype(jnp.float32) + projected).astype(jnp.bfloat16)
    widened = attended.astype(jnp.float32)
    normed = (widened * lax.rsqrt(lax.optimization_barrier(jnp.mean(widened * widened, axis=1, keepdims=True)) + 1e-06) * norm_gain).astype(jnp.bfloat16)
    groups = TOKENS // ROWS
    buffers, combiners = lax.map(lambda packed: route_block(packed[0], packed[1], packed[2]), (expert_ids.reshape(groups, ROWS, TOPK), gate_weights.reshape(groups, ROWS, TOPK), normed.reshape(groups, ROWS, D)))
    quarter_width = FF // N_GRP

    def run_expert(packed):
        rows_in, gate_block, up_block, down_block = packed
        flat_rows = rows_in.reshape(groups * CAP, D)
        summed = jnp.zeros((groups * CAP, D), jnp.float32)
        for quarter in range(N_GRP):
            lower_col = quarter * quarter_width
            upper_col = lower_col + quarter_width
            gate_part = jnp.dot(flat_rows, gate_block[:, lower_col:upper_col], preferred_element_type=jnp.float32)
            up_part = jnp.dot(flat_rows, up_block[:, lower_col:upper_col], preferred_element_type=jnp.float32)
            hidden = (jax.nn.silu(gate_part) * up_part).astype(jnp.bfloat16)
            part_out = jnp.dot(hidden, down_block[lower_col:upper_col], preferred_element_type=jnp.float32).astype(jnp.bfloat16)
            summed = summed + part_out.astype(jnp.float32)
        return summed.astype(jnp.bfloat16).reshape(groups, CAP, D)
    expert_out = lax.map(run_expert, (jnp.swapaxes(buffers, 0, 1), gate_proj, up_proj, down_proj))
    returned = jnp.swapaxes(expert_out, 0, 1).reshape(groups, E * CAP, D)
    expert_mix = lax.map(lambda packed: jnp.dot(packed[0], packed[1], preferred_element_type=jnp.float32), (combiners, returned))
    layer_out = (widened + expert_mix.reshape(TOKENS, D)).astype(jnp.bfloat16)
    return (attended, layer_out)
```

```python
import jax
import jax.numpy as jnp
from jax import lax
from jax.sharding import PartitionSpec as P

D = 2048
HD = 128
E = 64
TOPK = 6
SLOTS = 16
FAR = [(0, 3), (3, 0), (1, 2), (2, 1)]
NEAR = [(0, 1), (1, 0), (2, 3), (3, 2)]
F32 = jnp.float32
BF16 = jnp.bfloat16


def feature_map(values):
    return (jax.nn.elu(values.astype(F32)) + 1.0).astype(BF16)


def hi_lo(x):
    hi = x.astype(BF16)
    lo = (x - hi.astype(F32)).astype(BF16)
    return hi, lo


def prior_of(block_total, shard_state, local_norm):
    n = lax.axis_size("ctx")
    heads = shard_state.shape[0]
    per_head = n // heads
    rows = shard_state.astype(BF16).reshape(n, SLOTS, HD)
    norm_hi, norm_lo = hi_lo(local_norm.reshape(n, SLOTS))
    tot = jnp.repeat(block_total, per_head)[:, None]
    tot_hi, tot_lo = hi_lo(tot)
    tot_lo2 = (tot - tot_hi.astype(F32) - tot_lo.astype(F32)).astype(BF16)
    extra = jnp.concatenate([norm_hi, norm_lo, tot_hi, tot_lo, tot_lo2], axis=1)
    extra = jnp.pad(extra, ((0, 0), (0, HD - extra.shape[1])))[:, None, :]
    payload = jnp.concatenate([rows, jnp.pad(extra, ((0, 0), (0, 7), (0, 0)))], axis=1)
    got = lax.all_to_all(payload, "ctx", 0, 0, tiled=True)
    line = got[:, SLOTS, :].astype(F32)
    totals = line[:, 32] + line[:, 33] + line[:, 34]
    later = jnp.arange(n)
    between = (later[None, None, :] > later[None, :, None]) & (
        later[None, None, :] < later[:, None, None]
    )
    spread = jnp.sum(jnp.where(between, totals[None, None, :], 0.0), axis=2)
    mixer = jnp.where(later[None, :] < later[:, None], jnp.exp(spread), 0.0)
    states = jnp.einsum(
        "bk,krv->brv", mixer, got[:, :SLOTS, :].astype(F32), precision=lax.Precision.HIGHEST
    )
    norms = jnp.dot(mixer, line[:, :16] + line[:, 16:32], precision=lax.Precision.HIGHEST)
    n_hi, n_lo = hi_lo(norms)
    back_extra = jnp.pad(jnp.concatenate([n_hi, n_lo], axis=1), ((0, 0), (0, HD - 32)))[:, None, :]
    back = jnp.concatenate(
        [states.astype(BF16), jnp.pad(back_extra, ((0, 0), (0, 7), (0, 0)))], axis=1
    )
    mine = lax.all_to_all(back, "ctx", 0, 0, tiled=True)
    state = mine[:, :SLOTS, :].reshape(heads, HD, HD)
    ln = mine[:, SLOTS, :].astype(F32)
    norm = (ln[:, :16] + ln[:, 16:32]).reshape(heads, HD)
    return state, norm


def half_ffn(x, gate, up, down):
    a = lax.dot_general(x, gate, (((1,), (1,)), ((), ())), preferred_element_type=F32)
    b = lax.dot_general(x, up, (((1,), (1,)), ((), ())), preferred_element_type=F32)
    hidden = (jax.nn.silu(a) * b).astype(BF16)
    return jnp.dot(hidden, down, preferred_element_type=F32)


def on_device(
    query_heads,
    key_heads,
    value_heads,
    log_decay,
    residual,
    out_weight,
    norm_gain,
    expert_ids,
    gate_weights,
    gate_proj,
    up_proj,
    down_proj,
):
    n_ctx = lax.axis_size("ctx")
    gate_t = jnp.swapaxes(gate_proj, 1, 2)
    up_t = jnp.swapaxes(up_proj, 1, 2)
    pairs = ((NEAR, FAR), (FAR, NEAR))
    weights = []
    for which in range(2):
        weights.append(
            [
                jnp.concatenate([w[which], lax.ppermute(w[which], "grp", pairs[which][0])], axis=0)
                for w in (gate_t, up_t, down_proj)
            ]
        )

    length = query_heads.shape[0]
    local_heads = query_heads.shape[1] // HD
    feat_query = feature_map(query_heads).reshape(length, local_heads, HD)
    feat_key = feature_map(key_heads).reshape(length, local_heads, HD)
    value_rows = value_heads.reshape(length, local_heads, HD)
    cumulative = jnp.cumsum(log_decay, axis=1)
    block_total = cumulative[:, -1]
    tail = feat_key.astype(F32) * jnp.exp(block_total[:, None] - cumulative).T[:, :, None]
    shard_state = jnp.einsum(
        "jfi,jfx->fix", tail.astype(BF16), value_rows, preferred_element_type=F32
    )
    local_norm = jnp.sum(tail, axis=0)
    prior_state, prior_norm = prior_of(block_total, shard_state, local_norm)

    scores = jnp.einsum("thd,shd->hts", feat_query, feat_key, preferred_element_type=F32)
    row_index = lax.broadcasted_iota(jnp.int32, (length, length), 0)
    col_index = lax.broadcasted_iota(jnp.int32, (length, length), 1)
    causal = (col_index <= row_index)[None]
    spread = cumulative[:, :, None] - cumulative[:, None, :]
    w = jnp.where(causal, scores * jnp.exp(jnp.where(causal, spread, 0.0)), 0.0)
    inner_den = jnp.sum(w, axis=2).T
    inner_num = jnp.einsum("hts,shd->thd", w.astype(BF16), value_rows, preferred_element_type=F32)
    damp = jnp.exp(cumulative).T
    outer_num = damp[:, :, None] * jnp.einsum(
        "thn,hnp->thp", feat_query, prior_state, preferred_element_type=F32
    )
    outer_den = damp * jnp.sum(feat_query.astype(F32) * prior_norm[None], axis=2)
    mixed = ((inner_num + outer_num) / (inner_den + outer_den)[:, :, None]).astype(BF16)

    n_grp = lax.axis_size("grp")
    mixed = mixed.reshape(n_grp, length // n_grp, local_heads * HD)
    heads_in = lax.all_to_all(mixed, "grp", 0, 0, tiled=True)
    projected = jnp.einsum(
        "gtc,gcd->td", heads_in, out_weight.reshape(n_grp, -1, D), preferred_element_type=F32
    )
    attended = (residual.astype(F32) + projected).astype(BF16)
    widened = attended.astype(F32)
    normed = (
        widened * lax.rsqrt(jnp.mean(widened * widened, axis=1, keepdims=True) + 1e-06) * norm_gain
    ).astype(BF16)

    row_count = expert_ids.shape[0]
    onehot = (expert_ids[:, :, None] == jnp.arange(E, dtype=jnp.int32)).astype(jnp.int32)
    flat_hits = onehot.reshape(row_count * TOPK, E)
    earlier = jnp.cumsum(flat_hits, axis=0) - flat_hits
    slot_index = jnp.sum(earlier * flat_hits, axis=1).reshape(row_count, TOPK)
    target = (expert_ids % 2) * (n_ctx * SLOTS) + (expert_ids // 2) * SLOTS + slot_index
    gates = gate_weights.astype(BF16).astype(F32)

    sent = []
    combiners = []
    for which in range(2):
        places = jnp.arange(n_ctx * SLOTS, dtype=jnp.int32) + which * n_ctx * SLOTS
        placed = (target[:, :, None] == places).astype(F32)
        dispatch = jnp.sum(placed, axis=1).astype(BF16)
        combiners.append(jnp.sum(placed * gates[:, :, None], axis=1).astype(BF16))
        buffer = jnp.einsum("rs,rd->sd", dispatch, normed, preferred_element_type=F32).astype(BF16)
        sent.append(
            lax.all_to_all(buffer.reshape(n_ctx, SLOTS, D), "ctx", 0, 0, tiled=True)
        )
    total = widened
    backs = []
    for which in range(2):
        own = sent[which].reshape(n_ctx * SLOTS, D)
        other = lax.ppermute(own, "grp", pairs[which][1])
        own_out = half_ffn(own, *weights[which])
        other_out = half_ffn(other, *weights[which]).astype(BF16)
        came = lax.ppermute(other_out, "grp", pairs[which][1])
        summed = (own_out + came.astype(F32)).astype(BF16)
        backs.append(
            lax.all_to_all(summed.reshape(n_ctx, SLOTS, D), "ctx", 0, 0, tiled=True)
        )
    for which in range(2):
        total = total + jnp.dot(
            combiners[which], backs[which].reshape(-1, D), preferred_element_type=F32
        )
    return (attended, total.astype(BF16))


def solution(mesh):
    placed = (
        P("ctx", "grp"),
        P("ctx", "grp"),
        P("ctx", "grp"),
        P("grp", "ctx"),
        P(("ctx", "grp"), None),
        P(),
        P(),
        P(("ctx", "grp"), None),
        P(("ctx", "grp"), None),
        P("ctx", None, "grp"),
        P("ctx", None, "grp"),
        P("ctx", "grp", None),
    )
    return jax.shard_map(
        on_device,
        mesh=mesh,
        in_specs=placed,
        out_specs=(P(("ctx", "grp"), None), P(("ctx", "grp"), None)),
        check_vma=False,
    )
```

```python
import functools

import jax
import jax.numpy as jnp
from jax import lax
from jax.experimental import pallas as pl
from jax.experimental.pallas import tpu as pltpu
from jax.sharding import PartitionSpec as P


D = 2048
HD = 128
E = 64
TOPK = 6
SLOTS = 16
CHUNKS = 2
EXTRA = 8
GRANT = 58 << 20
FAR = [(0, 3), (3, 0), (1, 2), (2, 1)]
NEAR = [(0, 1), (1, 0), (2, 3), (3, 2)]
F32 = jnp.float32
BF16 = jnp.bfloat16


def feature(values):
    wide = values.astype(F32)
    return jnp.where(wide > 0, wide + 1.0, jnp.exp(jnp.minimum(wide, 0.0))).astype(BF16)


def running_sum(rows):
    lanes = lax.broadcasted_iota(jnp.int32, rows.shape, 1)
    step = 1
    while step < rows.shape[1]:
        rows = rows + jnp.where(lanes >= step, pltpu.roll(rows, step, 1), 0.0)
        step *= 2
    return rows


def padded_decay(decay_ref):
    decay = decay_ref[...]
    return jnp.concatenate([decay, jnp.zeros((8 - decay.shape[0], decay.shape[1]), F32)], axis=0)


def state_body(k_ref, v_ref, decay_ref, out_ref):
    heads, length = decay_ref.shape
    cum = running_sum(padded_decay(decay_ref))
    total = cum[:, length - 1 :]
    fade = jnp.exp(total - cum).T
    parts = out_ref.shape[0] // heads
    row = lax.broadcasted_iota(jnp.int32, (EXTRA, HD), 0)
    for h in range(heads):
        cols = slice(h * HD, (h + 1) * HD)
        tail = feature(k_ref[:, cols]).astype(F32) * fade[:, h : h + 1]
        norm = jnp.sum(tail, axis=0, keepdims=True)
        state = lax.dot_general(
            tail.astype(BF16), v_ref[:, cols], (((0,), (0,)), ((), ())), preferred_element_type=F32
        )
        out_ref[h * parts : (h + 1) * parts, 0:SLOTS, :] = state.astype(BF16).reshape(
            parts, SLOTS, HD
        )
        norm_hi = norm.astype(BF16).astype(F32)
        tot = jnp.broadcast_to(total[h : h + 1, :], (1, HD))
        tot_hi = tot.astype(BF16).astype(F32)
        tot_lo = (tot - tot_hi).astype(BF16).astype(F32)
        extra = jnp.zeros((EXTRA, HD), F32)
        for i, line in enumerate((norm_hi, norm - norm_hi, tot_hi, tot_lo, tot - tot_hi - tot_lo)):
            extra = jnp.where(row == i, line, extra)
        out_ref[h * parts : (h + 1) * parts, SLOTS:, :] = jnp.broadcast_to(
            extra.astype(BF16)[None], (parts, EXTRA, HD)
        )


def local_states(keys, values, decay, blocks):
    return pl.pallas_call(
        state_body,
        out_shape=jax.ShapeDtypeStruct((blocks, SLOTS + EXTRA, HD), BF16),
        compiler_params=pltpu.CompilerParams(vmem_limit_bytes=GRANT),
        name="local_states",
    )(keys, values, decay)


def prior_body(got_ref, out_ref):
    blocks = got_ref.shape[0]
    row = lax.broadcasted_iota(jnp.int32, (EXTRA, HD), 0)

    def step(b, carry):
        state, norm = carry
        extra = got_ref[b, SLOTS:, :].astype(F32)

        def line(i):
            return jnp.sum(jnp.where(row == i, extra, 0.0), axis=0, keepdims=True)

        norm_hi = norm.astype(BF16).astype(F32)
        out_ref[b, 0:SLOTS, :] = state.astype(BF16)
        out_ref[b, SLOTS:, :] = jnp.where(
            row == 0, norm_hi, jnp.where(row == 1, norm - norm_hi, 0.0)
        ).astype(BF16)
        fade = jnp.exp(line(2) + line(3) + line(4))
        state = fade * state + got_ref[b, 0:SLOTS, :].astype(F32)
        norm = fade * norm + line(0) + line(1)
        return state, norm

    lax.fori_loop(
        0, blocks, step, (jnp.zeros((SLOTS, HD), F32), jnp.zeros((1, HD), F32)), unroll=4
    )


def prior_states(got):
    return pl.pallas_call(
        prior_body, out_shape=jax.ShapeDtypeStruct(got.shape, BF16), compiler_params=pltpu.CompilerParams(vmem_limit_bytes=4 << 20),
        name="prior_states"
    )(got)


def inner_body(q_ref, k_ref, v_ref, decay_ref, num_ref, den_ref):
    heads, length = decay_ref.shape
    cum = running_sum(padded_decay(decay_ref))
    cum_col = cum.T
    tile = 128
    lane = lax.broadcasted_iota(jnp.int32, (tile, HD), 1)
    for t in range(length // tile):
        rows = slice(t * tile, (t + 1) * tile)
        seen = (t + 1) * tile
        col = lax.broadcasted_iota(jnp.int32, (tile, seen), 1)
        at = lax.broadcasted_iota(jnp.int32, (tile, seen), 0) + t * tile
        causal = col <= at
        dens = jnp.zeros((tile, HD), F32)
        for h in range(heads):
            cols = slice(h * HD, (h + 1) * HD)
            scores = lax.dot_general(
                feature(q_ref[rows, cols]),
                feature(k_ref[0:seen, cols]),
                (((1,), (1,)), ((), ())),
                preferred_element_type=F32,
            )
            spread = cum_col[rows, h : h + 1] - cum[h : h + 1, 0:seen]
            weights = jnp.where(causal, scores * jnp.exp(jnp.where(causal, spread, 0.0)), 0.0)
            dens = jnp.where(lane == h, jnp.sum(weights, axis=1, keepdims=True), dens)
            num_ref[rows, cols] = jnp.dot(
                weights.astype(BF16), v_ref[0:seen, cols], preferred_element_type=F32
            )
        den_ref[rows, :] = dens


def inner_attention(queries, keys, values, decay):
    length, width = queries.shape
    return pl.pallas_call(
        inner_body,
        out_shape=[
            jax.ShapeDtypeStruct((length, width), F32),
            jax.ShapeDtypeStruct((length, HD), F32),
        ],
        cost_estimate=pl.CostEstimate(
            flops=4 * length * length * width,
            bytes_accessed=8 * length * width,
            transcendentals=4 * length * length,
        ),
        compiler_params=pltpu.CompilerParams(vmem_limit_bytes=GRANT),
        name="inner_attention",
    )(queries, keys, values, decay)


def outer_body(q_ref, decay_ref, prior_ref, num_ref, den_ref, out_ref):
    heads, length = decay_ref.shape
    groups = out_ref.shape[0]
    parts = prior_ref.shape[0] // heads
    damp = jnp.exp(running_sum(padded_decay(decay_ref))).T
    row = lax.broadcasted_iota(jnp.int32, (EXTRA, HD), 0)
    for h in range(heads):
        cols = slice(h * HD, (h + 1) * HD)
        feat = feature(q_ref[:, cols])
        state = prior_ref[h * parts : (h + 1) * parts, 0:SLOTS, :].reshape(HD, HD)
        extra = prior_ref[h * parts, SLOTS:, :].astype(F32)
        norm = jnp.sum(jnp.where(row < 2, extra, 0.0), axis=0, keepdims=True)
        scale = damp[:, h : h + 1]
        num = num_ref[:, cols] + scale * jnp.dot(feat, state, preferred_element_type=F32)
        den = den_ref[:, h : h + 1] + scale * jnp.sum(
            feat.astype(F32) * norm, axis=1, keepdims=True
        )
        out_ref[:, :, cols] = (num / den).astype(BF16).reshape(groups, length // groups, HD)


def outer_attention(queries, decay, prior, num, den, groups):
    length, width = queries.shape
    return pl.pallas_call(
        outer_body,
        out_shape=jax.ShapeDtypeStruct((groups, length // groups, width), BF16),
        compiler_params=pltpu.CompilerParams(vmem_limit_bytes=GRANT),
        name="outer_attention",
    )(queries, decay, prior, num, den)


def route_body(ids_ref, gates_ref, dispatch_ref, combine_ref, even_ref, odd_ref):
    rows = ids_ref.shape[1]
    expert = lax.broadcasted_iota(jnp.int32, (E, rows), 0)
    hits = jnp.zeros((E, rows), F32)
    gates = jnp.zeros((E, rows), F32)
    for k in range(TOPK):
        match = expert == ids_ref[k : k + 1, :]
        hits = jnp.where(match, 1.0, hits)
        gates = jnp.where(match, gates_ref[k : k + 1, :], gates)
    before = (
        lax.broadcasted_iota(jnp.int32, (rows, rows), 0)
        < lax.broadcasted_iota(jnp.int32, (rows, rows), 1)
    ).astype(BF16)
    slot = jnp.dot(hits.astype(BF16), before, preferred_element_type=F32)
    slot = jnp.where(hits > 0.0, slot, -1.0)
    gates = gates.astype(BF16).astype(F32)
    half = SLOTS // CHUNKS
    for chunk in range(CHUNKS):
        place = lax.broadcasted_iota(jnp.int32, (E, half, rows), 1) + chunk * half
        here = jnp.broadcast_to(slot[:, None, :], (E, half, rows)) == place.astype(F32)
        dispatch_ref[chunk] = jnp.where(here, 1.0, 0.0).reshape(E * half, rows).astype(BF16)
        mix = jnp.where(here, jnp.broadcast_to(gates[:, None, :], (E, half, rows)), 0.0)
        combine_ref[chunk] = mix.reshape(E * half, rows).astype(BF16)
        if chunk == 0:
            by_parity = mix.reshape(E // 2, 2, half, rows)
            for parity, ref in ((0, even_ref), (1, odd_ref)):
                ref[...] = by_parity[:, parity].reshape(E // 2 * half, rows).astype(BF16)


def route(ids, gates):
    rows = ids.shape[1]
    shape = jax.ShapeDtypeStruct((CHUNKS, E * SLOTS // CHUNKS, rows), BF16)
    part = jax.ShapeDtypeStruct((E // 2 * SLOTS // CHUNKS, rows), BF16)
    return pl.pallas_call(
        route_body,
        out_shape=[shape, shape, part, part], compiler_params=pltpu.CompilerParams(vmem_limit_bytes=4 << 20),
        name="route",
    )(ids, gates)


def contract_last(x, y):
    return lax.dot_general(x, y, (((1,), (1,)), ((), ())), preferred_element_type=F32)


def apply_half(x, weights, store, waits):
    waits(0)
    gate = contract_last(x, weights[0])
    waits(1)
    up = contract_last(x, weights[1])
    hidden = (jax.nn.silu(gate) * up).astype(BF16)
    waits(2)
    width = D // 4

    def down(i, carry):
        at = pl.multiple_of(i * width, width)
        store(at, width, jnp.dot(hidden, weights[2, :, pl.ds(at, width)], preferred_element_type=F32))
        return carry

    lax.fori_loop(0, 4, down, 0)


def single_body(which, x_ref, g_ref, u_ref, d_ref, gf, uf, df, out_ref, xs, ws, sems):
    quarter = gf.shape[0]
    copies = []
    for i, (own, far) in enumerate(((g_ref, gf), (u_ref, uf), (d_ref, df))):
        copies.append(
            (
                pltpu.make_async_copy(own.at[which], ws.at[i, 0:quarter], sems.at[2 * i]),
                pltpu.make_async_copy(far, ws.at[i, quarter : 2 * quarter], sems.at[2 * i + 1]),
            )
        )
    x_copy = pltpu.make_async_copy(x_ref, xs, sems.at[6])
    x_copy.start()
    for pair in copies:
        for copy in pair:
            copy.start()
    x_copy.wait()

    def waits(i):
        for copy in copies[i]:
            copy.wait()

    def store(at, width, value):
        out_ref[:, pl.ds(at, width)] = value.astype(BF16)

    apply_half(xs[...].reshape(-1, D), ws, store, waits)


def single_ffn(x, own, far, which):
    quarter = far[0].shape[0]
    blocks, rows, _ = x.shape
    total = blocks * rows
    anywhere = pl.BlockSpec(memory_space=pl.ANY)
    held = pl.BlockSpec(memory_space=pltpu.HBM)
    return pl.pallas_call(
        functools.partial(single_body, which),
        out_shape=jax.ShapeDtypeStruct((total, D), BF16),
        in_specs=[anywhere] + [held] * 6,
        out_specs=pl.BlockSpec(memory_space=pltpu.VMEM),
        scratch_shapes=[
            pltpu.VMEM((blocks, rows, D), BF16),
            pltpu.VMEM((3, 2 * quarter, D), BF16),
            pltpu.SemaphoreType.DMA((7,)),
        ],
        compiler_params=pltpu.CompilerParams(vmem_limit_bytes=GRANT),
        cost_estimate=pl.CostEstimate(
            flops=12 * total * quarter * D,
            bytes_accessed=12 * quarter * D + 4 * total * D,
            transcendentals=2 * total * quarter,
        ),
        name="single_ffn",
    )(x, *own, *far)


def pair_body(starts, xa, xb, g_ref, u_ref, d_ref, ga, ua, da, gb, ub, db, out_ref, xs, ws, sems):
    quarter = ga.shape[0]
    blocks, rows, _ = out_ref.shape
    rows = rows // 2
    for e, (x_ref, fars) in enumerate(((xa, (ga, ua, da)), (xb, (gb, ub, db)))):
        pltpu.make_async_copy(
            x_ref.at[:, starts[e] : starts[e] + rows, :], xs.at[e], sems.at[7 * e + 6]
        ).start()
        for i, (own, far) in enumerate(zip((g_ref, u_ref, d_ref), fars)):
            pair = (
                pltpu.make_async_copy(own.at[e], ws.at[e, i, 0:quarter], sems.at[7 * e + 2 * i]),
                pltpu.make_async_copy(
                    far, ws.at[e, i, quarter : 2 * quarter], sems.at[7 * e + 2 * i + 1]
                ),
            )
            for copy in pair:
                copy.start()

    def expert(e, carry):
        def wait_for(ref, dst, sem):
            pltpu.make_async_copy(ref, dst, sems.at[7 * e + sem]).wait()

        wait_for(xa.at[:, 0:rows, :], xs.at[e], 6)

        def waits(i):
            wait_for(ga, ws.at[e, i, 0:quarter], 2 * i)
            wait_for(ga, ws.at[e, i, quarter : 2 * quarter], 2 * i + 1)

        def store(at, width, value):
            where = pl.ds(pl.multiple_of(e * rows, rows), rows)
            out_ref[:, where, pl.ds(at, width)] = value.astype(BF16).reshape(blocks, rows, width)

        apply_half(xs[e].reshape(-1, D), ws.at[e], store, waits)
        return carry

    lax.fori_loop(0, 2, expert, 0)


def pair_ffn(xa, xb, starts, own, fars):
    quarter = fars[0][0].shape[0]
    blocks = xa.shape[0]
    rows = SLOTS // CHUNKS
    total = 2 * blocks * rows
    anywhere = pl.BlockSpec(memory_space=pl.ANY)
    held = pl.BlockSpec(memory_space=pltpu.HBM)
    return pl.pallas_call(
        functools.partial(pair_body, starts),
        out_shape=jax.ShapeDtypeStruct((blocks, 2 * rows, D), BF16),
        in_specs=[anywhere] * 2 + [held] * 9,
        out_specs=pl.BlockSpec(memory_space=pltpu.VMEM),
        scratch_shapes=[
            pltpu.VMEM((2, blocks, rows, D), BF16),
            pltpu.VMEM((2, 3, 2 * quarter, D), BF16),
            pltpu.SemaphoreType.DMA((14,)),
        ],
        compiler_params=pltpu.CompilerParams(vmem_limit_bytes=GRANT),
        cost_estimate=pl.CostEstimate(
            flops=12 * total * quarter * D,
            bytes_accessed=24 * quarter * D + 4 * total * D,
            transcendentals=2 * total * quarter,
        ),
        name="pair_ffn",
    )(xa, xb, *own, *fars[0], *fars[1])


def merge_body(own, came_a, came_b, out):
    blocks, rows, _ = out.shape
    rows = rows // 2
    for at, came in ((0, came_a), (rows, came_b)):
        back = came[...].astype(F32).reshape(blocks, rows, D)
        out[:, at : at + rows, :] = (own[:, at : at + rows, :].astype(F32) + back).astype(BF16)


def merge(own, came_a, came_b):
    blocks, rows, _ = own.shape
    steps = 4
    wide = pl.BlockSpec((blocks // steps, rows, D), lambda i: (i, 0, 0))
    flat = pl.BlockSpec((came_a.shape[0] // steps, D), lambda i: (i, 0))
    return pl.pallas_call(
        merge_body,
        grid=(steps,),
        out_shape=jax.ShapeDtypeStruct(own.shape, BF16),
        in_specs=[wide, flat, flat],
        out_specs=wide,
        compiler_params=pltpu.CompilerParams(vmem_limit_bytes=16 << 20),
        cost_estimate=pl.CostEstimate(
            flops=blocks * rows * D, bytes_accessed=6 * blocks * rows * D, transcendentals=0
        ),
        name="merge",
    )(own, came_a, came_b)


def partner_body(back, mix_a, mix_b, far_ref, near_ref):
    blocks, rows, width = back.shape
    rows = rows // 2
    for at, mix, out in ((0, mix_a, far_ref), (rows, mix_b, near_ref)):
        part = back[:, at : at + rows, :].reshape(blocks * rows, width)
        out[...] = lax.dot_general(
            mix[...], part, (((0,), (0,)), ((), ())), preferred_element_type=F32
        ).astype(BF16)


def partner_mix(back, mix_a, mix_b):
    blocks, rows, _ = back.shape
    tokens = mix_a.shape[1]
    steps = 4
    out = jax.ShapeDtypeStruct((tokens, D), BF16)
    whole = pl.BlockSpec(mix_a.shape, lambda i: (0, 0))
    strip = pl.BlockSpec((tokens, D // steps), lambda i: (0, i))
    return pl.pallas_call(
        partner_body,
        grid=(steps,),
        out_shape=[out, out],
        in_specs=[
            pl.BlockSpec((blocks, rows, D // steps), lambda i: (0, 0, i)),
            whole,
            whole,
        ],
        out_specs=[strip, strip],
        compiler_params=pltpu.CompilerParams(vmem_limit_bytes=16 << 20),
        cost_estimate=pl.CostEstimate(
            flops=2 * blocks * rows * tokens * D,
            bytes_accessed=2 * blocks * rows * D,
            transcendentals=0,
        ),
        name="partner_mix",
    )(back, mix_a, mix_b)


def on_device(
    query_heads,
    key_heads,
    value_heads,
    log_decay,
    residual,
    out_weight,
    norm_gain,
    expert_ids,
    gate_weights,
    gate_proj,
    up_proj,
    down_proj,
):
    n_ctx = lax.axis_size("ctx")
    gate_t = jnp.swapaxes(gate_proj, 1, 2)
    up_t = jnp.swapaxes(up_proj, 1, 2)
    pairs = ((NEAR, FAR), (FAR, NEAR))
    own_w = (gate_t, up_t, down_proj)
    far_w = [[], []]
    for w in (gate_t, up_t, down_proj):
        for which in range(2):
            far_w[which].append(lax.ppermute(w[which], "grp", pairs[which][0]))

    n_grp = lax.axis_size("grp")
    payload = local_states(key_heads, value_heads, log_decay, n_ctx)
    got = lax.all_to_all(payload, "ctx", 0, 0, tiled=True)
    dispatch, combine, even, odd = route(jnp.swapaxes(expert_ids, 0, 1), jnp.swapaxes(gate_weights, 0, 1))
    far_even = lax.ppermute(even, "grp", FAR)
    near_odd = lax.ppermute(odd, "grp", NEAR)
    back = prior_states(got)
    prior = lax.all_to_all(back, "ctx", 0, 0, tiled=True)
    num, den = inner_attention(query_heads, key_heads, value_heads, log_decay)
    mixed = outer_attention(query_heads, log_decay, prior, num, den, n_grp)
    heads_in = lax.all_to_all(mixed, "grp", 0, 0, tiled=True)
    projected = jnp.einsum(
        "gtc,gcd->td", heads_in, out_weight.reshape(n_grp, -1, D), preferred_element_type=F32
    )
    attended = (residual.astype(F32) + projected).astype(BF16)
    widened = attended.astype(F32)
    normed = (
        widened * lax.rsqrt(jnp.mean(widened * widened, axis=1, keepdims=True) + 1e-06) * norm_gain
    ).astype(BF16)

    half = SLOTS // CHUNKS
    sent = []
    for chunk in range(CHUNKS):
        buffer = jnp.dot(dispatch[chunk], normed, preferred_element_type=F32).astype(BF16)
        sent.append(
            lax.all_to_all(buffer.reshape(n_ctx, 2 * half, D), "ctx", 0, 0, tiled=True)
        )
    others = []
    for chunk in range(CHUNKS):
        for which in range(2):
            own = sent[chunk][:, which * half : (which + 1) * half]
            others.append(lax.ppermute(own, "grp", pairs[which][1]))

    def home(rows):
        return lax.all_to_all(rows, "ctx", 0, 0, tiled=True)

    def mix(chunk, back):
        return lax.dot_general(
            combine[chunk],
            back.reshape(-1, D),
            (((0,), (0,)), ((), ())),
            preferred_element_type=F32,
        )

    own0 = pair_ffn(sent[0], sent[0], (0, half), own_w, far_w)
    back_own0 = home(own0)
    other0 = pair_ffn(others[0], others[1], (0, 0), own_w, far_w)
    back_other0 = home(other0)
    for_far, for_near = partner_mix(back_other0, far_even, near_odd)
    from_far = lax.ppermute(for_far, "grp", FAR)
    from_near = lax.ppermute(for_near, "grp", NEAR)

    own1 = pair_ffn(sent[1], sent[1], (0, half), own_w, far_w)
    came = []
    for which in range(2):
        other = single_ffn(others[2 + which], own_w, far_w[which], which)
        came.append(lax.ppermute(other, "grp", pairs[which][1]))
    back1 = home(merge(own1, *came))
    total = widened + mix(0, back_own0) + from_far.astype(F32) + from_near.astype(F32)
    total = total + mix(1, back1)
    return (attended, total.astype(BF16))


def solution(mesh):
    placed = (
        P("ctx", "grp"),
        P("ctx", "grp"),
        P("ctx", "grp"),
        P("grp", "ctx"),
        P(("ctx", "grp"), None),
        P(),
        P(),
        P(("ctx", "grp"), None),
        P(("ctx", "grp"), None),
        P("ctx", None, "grp"),
        P("ctx", None, "grp"),
        P("ctx", "grp", None),
    )

    return jax.shard_map(
        on_device,
        mesh=mesh,
        in_specs=placed,
        out_specs=(P(("ctx", "grp"), None), P(("ctx", "grp"), None)),
        check_vma=False,
    )
```

```python
import functools

import jax
import jax.numpy as jnp
from jax import lax
from jax.experimental import pallas as pl
from jax.experimental.pallas import tpu as pltpu
from jax.sharding import PartitionSpec as P


D = 2048
HD = 128
E = 64
TOPK = 6
SLOTS = 16
CHUNKS = 2
EXTRA = 8
GRANT = 58 << 20
KEEP_GRANT = 24 << 20
FAR = [(0, 3), (3, 0), (1, 2), (2, 1)]
NEAR = [(0, 1), (1, 0), (2, 3), (3, 2)]
F32 = jnp.float32
BF16 = jnp.bfloat16


def feature(values):
    wide = values.astype(F32)
    return jnp.where(wide > 0, wide + 1.0, jnp.exp(jnp.minimum(wide, 0.0))).astype(BF16)


def running_sum(rows):
    lanes = lax.broadcasted_iota(jnp.int32, rows.shape, 1)
    step = 1
    while step < rows.shape[1]:
        rows = rows + jnp.where(lanes >= step, pltpu.roll(rows, step, 1), 0.0)
        step *= 2
    return rows


def padded_decay(decay_ref):
    decay = decay_ref[...]
    return jnp.concatenate([decay, jnp.zeros((8 - decay.shape[0], decay.shape[1]), F32)], axis=0)


def state_body(k_ref, v_ref, decay_ref, out_ref):
    heads, length = decay_ref.shape
    cum = running_sum(padded_decay(decay_ref))
    total = cum[:, length - 1 :]
    fade = jnp.exp(total - cum).T
    parts = out_ref.shape[0] // heads
    row = lax.broadcasted_iota(jnp.int32, (EXTRA, HD), 0)
    for h in range(heads):
        cols = slice(h * HD, (h + 1) * HD)
        tail = feature(k_ref[:, cols]).astype(F32) * fade[:, h : h + 1]
        norm = jnp.sum(tail, axis=0, keepdims=True)
        state = lax.dot_general(
            tail.astype(BF16), v_ref[:, cols], (((0,), (0,)), ((), ())), preferred_element_type=F32
        )
        out_ref[h * parts : (h + 1) * parts, 0:SLOTS, :] = state.astype(BF16).reshape(
            parts, SLOTS, HD
        )
        norm_hi = norm.astype(BF16).astype(F32)
        tot = jnp.broadcast_to(total[h : h + 1, :], (1, HD))
        tot_hi = tot.astype(BF16).astype(F32)
        tot_lo = (tot - tot_hi).astype(BF16).astype(F32)
        extra = jnp.zeros((EXTRA, HD), F32)
        for i, line in enumerate((norm_hi, norm - norm_hi, tot_hi, tot_lo, tot - tot_hi - tot_lo)):
            extra = jnp.where(row == i, line, extra)
        out_ref[h * parts : (h + 1) * parts, SLOTS:, :] = jnp.broadcast_to(
            extra.astype(BF16)[None], (parts, EXTRA, HD)
        )


def local_states(keys, values, decay, blocks):
    return pl.pallas_call(
        state_body,
        out_shape=jax.ShapeDtypeStruct((blocks, SLOTS + EXTRA, HD), BF16),
        compiler_params=pltpu.CompilerParams(vmem_limit_bytes=8 << 20),
        name="local_states",
    )(keys, values, decay)


def prior_body(got_ref, out_ref):
    blocks = got_ref.shape[0]
    row = lax.broadcasted_iota(jnp.int32, (EXTRA, HD), 0)

    def step(b, carry):
        state, norm = carry
        extra = got_ref[b, SLOTS:, :].astype(F32)

        def line(i):
            return jnp.sum(jnp.where(row == i, extra, 0.0), axis=0, keepdims=True)

        norm_hi = norm.astype(BF16).astype(F32)
        out_ref[b, 0:SLOTS, :] = state.astype(BF16)
        out_ref[b, SLOTS:, :] = jnp.where(
            row == 0, norm_hi, jnp.where(row == 1, norm - norm_hi, 0.0)
        ).astype(BF16)
        fade = jnp.exp(line(2) + line(3) + line(4))
        state = fade * state + got_ref[b, 0:SLOTS, :].astype(F32)
        norm = fade * norm + line(0) + line(1)
        return state, norm

    lax.fori_loop(
        0, blocks, step, (jnp.zeros((SLOTS, HD), F32), jnp.zeros((1, HD), F32)), unroll=4
    )


def prior_states(got):
    return pl.pallas_call(
        prior_body, out_shape=jax.ShapeDtypeStruct(got.shape, BF16), compiler_params=pltpu.CompilerParams(vmem_limit_bytes=4 << 20),
        name="prior_states"
    )(got)


def inner_body(q_ref, k_ref, v_ref, decay_ref, num_ref, den_ref):
    heads, length = decay_ref.shape
    cum = running_sum(padded_decay(decay_ref))
    cum_col = cum.T
    tile = 128
    lane = lax.broadcasted_iota(jnp.int32, (tile, HD), 1)
    for t in range(length // tile):
        rows = slice(t * tile, (t + 1) * tile)
        seen = (t + 1) * tile
        col = lax.broadcasted_iota(jnp.int32, (tile, seen), 1)
        at = lax.broadcasted_iota(jnp.int32, (tile, seen), 0) + t * tile
        causal = col <= at
        dens = jnp.zeros((tile, HD), F32)
        for h in range(heads):
            cols = slice(h * HD, (h + 1) * HD)
            scores = lax.dot_general(
                feature(q_ref[rows, cols]),
                feature(k_ref[0:seen, cols]),
                (((1,), (1,)), ((), ())),
                preferred_element_type=F32,
            )
            spread = cum_col[rows, h : h + 1] - cum[h : h + 1, 0:seen]
            weights = jnp.where(causal, scores * jnp.exp(jnp.where(causal, spread, 0.0)), 0.0)
            dens = jnp.where(lane == h, jnp.sum(weights, axis=1, keepdims=True), dens)
            num_ref[rows, cols] = jnp.dot(
                weights.astype(BF16), v_ref[0:seen, cols], preferred_element_type=F32
            )
        den_ref[rows, :] = dens


def inner_attention(queries, keys, values, decay):
    length, width = queries.shape
    return pl.pallas_call(
        inner_body,
        out_shape=[
            jax.ShapeDtypeStruct((length, width), F32),
            jax.ShapeDtypeStruct((length, HD), F32),
        ],
        cost_estimate=pl.CostEstimate(
            flops=4 * length * length * width,
            bytes_accessed=8 * length * width,
            transcendentals=4 * length * length,
        ),
        compiler_params=pltpu.CompilerParams(vmem_limit_bytes=GRANT),
        name="inner_attention",
    )(queries, keys, values, decay)


def outer_body(q_ref, decay_ref, prior_ref, num_ref, den_ref, out_ref):
    heads, length = decay_ref.shape
    groups = out_ref.shape[0]
    parts = prior_ref.shape[0] // heads
    damp = jnp.exp(running_sum(padded_decay(decay_ref))).T
    row = lax.broadcasted_iota(jnp.int32, (EXTRA, HD), 0)
    for h in range(heads):
        cols = slice(h * HD, (h + 1) * HD)
        feat = feature(q_ref[:, cols])
        state = prior_ref[h * parts : (h + 1) * parts, 0:SLOTS, :].reshape(HD, HD)
        extra = prior_ref[h * parts, SLOTS:, :].astype(F32)
        norm = jnp.sum(jnp.where(row < 2, extra, 0.0), axis=0, keepdims=True)
        scale = damp[:, h : h + 1]
        num = num_ref[:, cols] + scale * jnp.dot(feat, state, preferred_element_type=F32)
        den = den_ref[:, h : h + 1] + scale * jnp.sum(
            feat.astype(F32) * norm, axis=1, keepdims=True
        )
        out_ref[:, :, cols] = (num / den).astype(BF16).reshape(groups, length // groups, HD)


def outer_attention(queries, decay, prior, num, den, groups):
    length, width = queries.shape
    return pl.pallas_call(
        outer_body,
        out_shape=jax.ShapeDtypeStruct((groups, length // groups, width), BF16),
        compiler_params=pltpu.CompilerParams(vmem_limit_bytes=GRANT),
        name="outer_attention",
    )(queries, decay, prior, num, den)


def route_body(ids_ref, gates_ref, dispatch_ref, combine_ref, even_ref, odd_ref):
    rows = ids_ref.shape[1]
    expert = lax.broadcasted_iota(jnp.int32, (E, rows), 0)
    hits = jnp.zeros((E, rows), F32)
    gates = jnp.zeros((E, rows), F32)
    for k in range(TOPK):
        match = expert == ids_ref[k : k + 1, :]
        hits = jnp.where(match, 1.0, hits)
        gates = jnp.where(match, gates_ref[k : k + 1, :], gates)
    before = (
        lax.broadcasted_iota(jnp.int32, (rows, rows), 0)
        < lax.broadcasted_iota(jnp.int32, (rows, rows), 1)
    ).astype(BF16)
    slot = jnp.dot(hits.astype(BF16), before, preferred_element_type=F32)
    slot = jnp.where(hits > 0.0, slot, -1.0)
    gates = gates.astype(BF16).astype(F32)
    half = SLOTS // CHUNKS
    for chunk in range(CHUNKS):
        place = lax.broadcasted_iota(jnp.int32, (E, half, rows), 1) + chunk * half
        here = jnp.broadcast_to(slot[:, None, :], (E, half, rows)) == place.astype(F32)
        dispatch_ref[chunk] = jnp.where(here, 1.0, 0.0).reshape(E * half, rows).astype(BF16)
        mix = jnp.where(here, jnp.broadcast_to(gates[:, None, :], (E, half, rows)), 0.0)
        combine_ref[chunk] = mix.reshape(E * half, rows).astype(BF16)
        if chunk == 0:
            by_parity = mix.reshape(E // 2, 2, half, rows)
            for parity, ref in ((0, even_ref), (1, odd_ref)):
                ref[...] = by_parity[:, parity].reshape(E // 2 * half, rows).astype(BF16)


def route(ids, gates):
    rows = ids.shape[1]
    shape = jax.ShapeDtypeStruct((CHUNKS, E * SLOTS // CHUNKS, rows), BF16)
    part = jax.ShapeDtypeStruct((E // 2 * SLOTS // CHUNKS, rows), BF16)
    return pl.pallas_call(
        route_body,
        out_shape=[shape, shape, part, part], compiler_params=pltpu.CompilerParams(vmem_limit_bytes=4 << 20),
        name="route",
    )(ids, gates)


NT = (((1,), (1,)), ((), ()))
TN = (((0,), (0,)), ((), ()))


def expert_rows(x, weights, e, ready, emit):
    ready(0)
    gate = lax.dot_general(weights[e, 0], x, NT, preferred_element_type=F32)
    ready(1)
    up = lax.dot_general(weights[e, 1], x, NT, preferred_element_type=F32)
    hidden = (jax.nn.silu(gate) * up).astype(BF16)
    ready(2)
    width = D // 4

    def down(i, inner):
        cols = pl.ds(pl.multiple_of(i * width, width), width)
        part = lax.dot_general(hidden, weights[e, 2, :, cols], TN, preferred_element_type=F32)
        emit(cols, part.astype(BF16))
        return inner

    lax.fori_loop(0, 4, down, 0)


def experts_body(sets, *refs):
    count = 1 + max(at for pair in sets for at, _ in pair)
    rows_in = refs[:count]
    own = refs[count : count + 3]
    fars = (refs[count + 3 : count + 6], refs[count + 6 : count + 9])
    outs = refs[count + 9 : count + 9 + len(sets)]
    ws, xs, sems = refs[-3:]
    quarter = fars[0][0].shape[0]
    _, n_sets, blocks, rows, _ = xs.shape
    for e in range(2):
        for j, pair in enumerate(sets):
            at, first = pair[e]
            source = rows_in[at].at[:, first : first + rows, :]
            pltpu.make_async_copy(source, xs.at[e, j], sems.at[e, 6 + j]).start()
        for i in range(3):
            low = ws.at[e, i, 0:quarter]
            high = ws.at[e, i, quarter : 2 * quarter]
            pltpu.make_async_copy(own[i].at[e], low, sems.at[e, 2 * i]).start()
            pltpu.make_async_copy(fars[e][i], high, sems.at[e, 2 * i + 1]).start()

    def expert(e, carry):
        def ready(i):
            for part in range(2):
                held = ws.at[e, i, part * quarter : (part + 1) * quarter]
                pltpu.make_async_copy(fars[0][0], held, sems.at[e, 2 * i + part]).wait()

        def emit(cols, part):
            at = pl.ds(pl.multiple_of(e * rows, rows), rows)
            part = part.reshape(n_sets, blocks, rows, part.shape[1])
            for j in range(n_sets):
                outs[j][:, at, cols] = part[j]

        for j in range(n_sets):
            pltpu.make_async_copy(
                rows_in[0].at[:, 0:rows, :], xs.at[e, j], sems.at[e, 6 + j]
            ).wait()
        expert_rows(xs[e].reshape(-1, D), ws, e, ready, emit)
        return carry

    lax.fori_loop(0, 2, expert, 0)


def expert_cost(total, quarter, loaded):
    return pl.CostEstimate(
        flops=12 * total * quarter * D,
        bytes_accessed=loaded * 24 * quarter * D + 4 * total * D,
        transcendentals=2 * total * quarter,
    )


def experts(xs, sets, own, fars, keep=False):
    quarter = fars[0][0].shape[0]
    blocks = xs[0].shape[0]
    rows = SLOTS // CHUNKS
    out_shape = [jax.ShapeDtypeStruct((blocks, 2 * rows, D), BF16)] * len(sets)
    anywhere = pl.BlockSpec(memory_space=pl.ANY)
    held = pltpu.VMEM((2, 3, 2 * quarter, D), BF16)
    scratch = [
        pltpu.VMEM((2, len(sets), blocks, rows, D), BF16),
        pltpu.SemaphoreType.DMA((2, 6 + len(sets))),
    ]
    return pl.pallas_call(
        functools.partial(experts_body, sets),
        out_shape=out_shape + [held] if keep else out_shape,
        in_specs=[anywhere] * (len(xs) + 9),
        scratch_shapes=scratch if keep else [held] + scratch,
        compiler_params=pltpu.CompilerParams(vmem_limit_bytes=KEEP_GRANT if keep else GRANT),
        cost_estimate=expert_cost(2 * blocks * rows * len(sets), quarter, 1),
        name="experts",
    )(*xs, *own, *fars[0], *fars[1])


def last_body(xa, xb, weights, out_a, out_b, xs, sems):
    outs = (out_a, out_b)
    for e, x_ref in enumerate((xa, xb)):
        pltpu.make_async_copy(x_ref, xs.at[e], sems.at[e]).start()

    def expert(e, carry):
        def emit(cols, part):
            for k in range(2):

                @pl.when(e == k)
                def _():
                    outs[k][:, cols] = part

        pltpu.make_async_copy(xa, xs.at[e], sems.at[e]).wait()
        expert_rows(xs[e].reshape(-1, D), weights, e, lambda i: None, emit)
        return carry

    lax.fori_loop(0, 2, expert, 0)


def last_experts(xa, xb, weights):
    blocks, rows, _ = xa.shape
    anywhere = pl.BlockSpec(memory_space=pl.ANY)
    on_chip = pl.BlockSpec(memory_space=pltpu.VMEM)
    return pl.pallas_call(
        last_body,
        out_shape=[jax.ShapeDtypeStruct((blocks * rows, D), BF16)] * 2,
        in_specs=[anywhere, anywhere, on_chip],
        scratch_shapes=[
            pltpu.VMEM((2, blocks, rows, D), BF16),
            pltpu.SemaphoreType.DMA((2,)),
        ],
        compiler_params=pltpu.CompilerParams(vmem_limit_bytes=KEEP_GRANT),
        cost_estimate=expert_cost(2 * blocks * rows, weights.shape[2] // 2, 0),
        name="last_experts",
    )(xa, xb, weights)


def merge_body(own, came_a, came_b, out):
    blocks, rows, _ = out.shape
    rows = rows // 2
    for at, came in ((0, came_a), (rows, came_b)):
        back = came[...].astype(F32).reshape(blocks, rows, D)
        out[:, at : at + rows, :] = (own[:, at : at + rows, :].astype(F32) + back).astype(BF16)


def merge(own, came_a, came_b):
    blocks, rows, _ = own.shape
    steps = 4
    wide = pl.BlockSpec((blocks // steps, rows, D), lambda i: (i, 0, 0))
    flat = pl.BlockSpec((came_a.shape[0] // steps, D), lambda i: (i, 0))
    return pl.pallas_call(
        merge_body,
        grid=(steps,),
        out_shape=jax.ShapeDtypeStruct(own.shape, BF16),
        in_specs=[wide, flat, flat],
        out_specs=wide,
        compiler_params=pltpu.CompilerParams(vmem_limit_bytes=16 << 20),
        cost_estimate=pl.CostEstimate(
            flops=blocks * rows * D, bytes_accessed=6 * blocks * rows * D, transcendentals=0
        ),
        name="merge",
    )(own, came_a, came_b)


def partner_body(back, mix_a, mix_b, far_ref, near_ref):
    blocks, rows, width = back.shape
    rows = rows // 2
    for at, mix, out in ((0, mix_a, far_ref), (rows, mix_b, near_ref)):
        part = back[:, at : at + rows, :].reshape(blocks * rows, width)
        out[...] = lax.dot_general(
            mix[...], part, (((0,), (0,)), ((), ())), preferred_element_type=F32
        ).astype(BF16)


def partner_mix(back, mix_a, mix_b):
    blocks, rows, _ = back.shape
    tokens = mix_a.shape[1]
    steps = 4
    out = jax.ShapeDtypeStruct((tokens, D), BF16)
    whole = pl.BlockSpec(mix_a.shape, lambda i: (0, 0))
    strip = pl.BlockSpec((tokens, D // steps), lambda i: (0, i))
    return pl.pallas_call(
        partner_body,
        grid=(steps,),
        out_shape=[out, out],
        in_specs=[
            pl.BlockSpec((blocks, rows, D // steps), lambda i: (0, 0, i)),
            whole,
            whole,
        ],
        out_specs=[strip, strip],
        compiler_params=pltpu.CompilerParams(vmem_limit_bytes=16 << 20),
        cost_estimate=pl.CostEstimate(
            flops=2 * blocks * rows * tokens * D,
            bytes_accessed=2 * blocks * rows * D,
            transcendentals=0,
        ),
        name="partner_mix",
    )(back, mix_a, mix_b)


def on_device(
    query_heads,
    key_heads,
    value_heads,
    log_decay,
    residual,
    out_weight,
    norm_gain,
    expert_ids,
    gate_weights,
    gate_proj,
    up_proj,
    down_proj,
):
    n_ctx = lax.axis_size("ctx")
    gate_t = jnp.swapaxes(gate_proj, 1, 2)
    up_t = jnp.swapaxes(up_proj, 1, 2)
    pairs = ((NEAR, FAR), (FAR, NEAR))
    own_w = (gate_t, up_t, down_proj)
    far_w = [[], []]
    for w in (gate_t, up_t, down_proj):
        for which in range(2):
            far_w[which].append(lax.ppermute(w[which], "grp", pairs[which][0]))

    n_grp = lax.axis_size("grp")
    payload = local_states(key_heads, value_heads, log_decay, n_ctx)
    got = lax.all_to_all(payload, "ctx", 0, 0, tiled=True)
    dispatch, combine, even, odd = route(jnp.swapaxes(expert_ids, 0, 1), jnp.swapaxes(gate_weights, 0, 1))
    far_even = lax.ppermute(even, "grp", FAR)
    near_odd = lax.ppermute(odd, "grp", NEAR)
    back = prior_states(got)
    prior = lax.all_to_all(back, "ctx", 0, 0, tiled=True)
    num, den = inner_attention(query_heads, key_heads, value_heads, log_decay)
    mixed = outer_attention(query_heads, log_decay, prior, num, den, n_grp)
    heads_in = lax.all_to_all(mixed, "grp", 0, 0, tiled=True)
    projected = jnp.einsum(
        "gtc,gcd->td", heads_in, out_weight.reshape(n_grp, -1, D), preferred_element_type=F32
    )
    attended = (residual.astype(F32) + projected).astype(BF16)
    widened = attended.astype(F32)
    normed = (
        widened * lax.rsqrt(jnp.mean(widened * widened, axis=1, keepdims=True) + 1e-06) * norm_gain
    ).astype(BF16)

    half = SLOTS // CHUNKS
    sent = []
    for chunk in range(CHUNKS):
        buffer = jnp.dot(dispatch[chunk], normed, preferred_element_type=F32).astype(BF16)
        sent.append(
            lax.all_to_all(buffer.reshape(n_ctx, 2 * half, D), "ctx", 0, 0, tiled=True)
        )
    others = []
    for chunk in range(CHUNKS):
        for which in range(2):
            own = sent[chunk][:, which * half : (which + 1) * half]
            others.append(lax.ppermute(own, "grp", pairs[which][1]))

    def home(rows):
        return lax.all_to_all(rows, "ctx", 0, 0, tiled=True)

    def mix(chunk, back):
        return lax.dot_general(
            combine[chunk],
            back.reshape(-1, D),
            (((0,), (0,)), ((), ())),
            preferred_element_type=F32,
        )

    (own0,) = experts((sent[0],), (((0, 0), (0, half)),), own_w, far_w)
    back_own0 = home(own0)
    own1, other0, held = experts(
        (sent[1], others[0], others[1]),
        (((0, 0), (0, half)), ((1, 0), (2, 0))),
        own_w,
        far_w,
        keep=True,
    )
    back_other0 = home(other0)
    for_far, for_near = partner_mix(back_other0, far_even, near_odd)
    from_far = lax.ppermute(for_far, "grp", FAR)
    from_near = lax.ppermute(for_near, "grp", NEAR)

    results = last_experts(others[2], others[3], held)
    came = []
    for which in range(2):
        came.append(lax.ppermute(results[which], "grp", pairs[which][1]))
    back1 = home(merge(own1, *came))
    so_far = lax.optimization_barrier(widened + mix(0, back_own0))
    total = so_far + from_far.astype(F32) + from_near.astype(F32) + mix(1, back1)
    return (attended, total.astype(BF16))


def solution(mesh):
    placed = (
        P("ctx", "grp"),
        P("ctx", "grp"),
        P("ctx", "grp"),
        P("grp", "ctx"),
        P(("ctx", "grp"), None),
        P(),
        P(),
        P(("ctx", "grp"), None),
        P(("ctx", "grp"), None),
        P("ctx", None, "grp"),
        P("ctx", None, "grp"),
        P("ctx", "grp", None),
    )

    return jax.shard_map(
        on_device,
        mesh=mesh,
        in_specs=placed,
        out_specs=(P(("ctx", "grp"), None), P(("ctx", "grp"), None)),
        check_vma=False,
    )
```

```python
import functools

import jax
import jax.numpy as jnp
from jax import lax
from jax.experimental import pallas as pl
from jax.experimental.pallas import tpu as pltpu
from jax.sharding import PartitionSpec as P


D = 2048
HD = 128
E = 64
TOPK = 6
SLOTS = 16
CHUNKS = 2
EXTRA = 8
GRANT = 58 << 20
KEEP_GRANT = 16 << 20
FAR = [(0, 3), (3, 0), (1, 2), (2, 1)]
NEAR = [(0, 1), (1, 0), (2, 3), (3, 2)]
F32 = jnp.float32
BF16 = jnp.bfloat16
ANYWHERE = pl.BlockSpec(memory_space=pl.ANY)
ON_CHIP = pl.BlockSpec(memory_space=pltpu.VMEM)


def feature(values):
    wide = values.astype(F32)
    return jnp.where(wide > 0, wide + 1.0, jnp.exp(jnp.minimum(wide, 0.0))).astype(BF16)


def running_sum(rows):
    lanes = lax.broadcasted_iota(jnp.int32, rows.shape, 1)
    step = 1
    while step < rows.shape[1]:
        rows = rows + jnp.where(lanes >= step, pltpu.roll(rows, step, 1), 0.0)
        step *= 2
    return rows


def padded_decay(decay_ref):
    decay = decay_ref[...]
    return jnp.concatenate([decay, jnp.zeros((8 - decay.shape[0], decay.shape[1]), F32)], axis=0)


class Parting:
    def __init__(self, both, parts, held, sems):
        self.load = pltpu.make_async_copy(both, held, sems.at[0])
        self.stores = [
            pltpu.make_async_copy(held.at[e], parts[e], sems.at[1 + e]) for e in range(2)
        ]
        self.load.start()

    def turn(self):
        self.load.wait()
        for store in self.stores:
            store.start()

    def finish(self):
        for store in self.stores:
            store.wait()


def parting_scratch(both):
    return [pltpu.VMEM(both.shape, BF16), pltpu.SemaphoreType.DMA((3,))]


def parts_of(both):
    return [jax.ShapeDtypeStruct(both.shape[1:], BF16)] * 2


def state_body(k_ref, v_ref, decay_ref, w_ref, out_ref, wa_ref, wb_ref, held, sems):
    parting = Parting(w_ref, (wa_ref, wb_ref), held, sems)
    heads, length = decay_ref.shape
    cum = running_sum(padded_decay(decay_ref))
    total = cum[:, length - 1 :]
    fade = jnp.exp(total - cum).T
    parts = out_ref.shape[0] // heads
    parting.turn()
    row = lax.broadcasted_iota(jnp.int32, (EXTRA, HD), 0)
    for h in range(heads):
        cols = slice(h * HD, (h + 1) * HD)
        tail = feature(k_ref[:, cols]).astype(F32) * fade[:, h : h + 1]
        norm = jnp.sum(tail, axis=0, keepdims=True)
        state = lax.dot_general(
            tail.astype(BF16), v_ref[:, cols], (((0,), (0,)), ((), ())), preferred_element_type=F32
        )
        out_ref[h * parts : (h + 1) * parts, 0:SLOTS, :] = state.astype(BF16).reshape(
            parts, SLOTS, HD
        )
        norm_hi = norm.astype(BF16).astype(F32)
        tot = jnp.broadcast_to(total[h : h + 1, :], (1, HD))
        tot_hi = tot.astype(BF16).astype(F32)
        tot_lo = (tot - tot_hi).astype(BF16).astype(F32)
        extra = jnp.zeros((EXTRA, HD), F32)
        for i, line in enumerate((norm_hi, norm - norm_hi, tot_hi, tot_lo, tot - tot_hi - tot_lo)):
            extra = jnp.where(row == i, line, extra)
        out_ref[h * parts : (h + 1) * parts, SLOTS:, :] = jnp.broadcast_to(
            extra.astype(BF16)[None], (parts, EXTRA, HD)
        )
    parting.finish()


def local_states(keys, values, decay, blocks, both):
    return pl.pallas_call(
        state_body,
        out_shape=[jax.ShapeDtypeStruct((blocks, SLOTS + EXTRA, HD), BF16), *parts_of(both)],
        in_specs=[ON_CHIP] * 3 + [ANYWHERE],
        out_specs=[ON_CHIP, ANYWHERE, ANYWHERE],
        scratch_shapes=parting_scratch(both),
        compiler_params=pltpu.CompilerParams(vmem_limit_bytes=GRANT),
        name="local_states",
    )(keys, values, decay, both)


def prior_body(got_ref, out_ref):
    blocks = got_ref.shape[0]
    row = lax.broadcasted_iota(jnp.int32, (EXTRA, HD), 0)

    def step(b, carry):
        state, norm = carry
        extra = got_ref[b, SLOTS:, :].astype(F32)

        def line(i):
            return jnp.sum(jnp.where(row == i, extra, 0.0), axis=0, keepdims=True)

        norm_hi = norm.astype(BF16).astype(F32)
        out_ref[b, 0:SLOTS, :] = state.astype(BF16)
        out_ref[b, SLOTS:, :] = jnp.where(
            row == 0, norm_hi, jnp.where(row == 1, norm - norm_hi, 0.0)
        ).astype(BF16)
        fade = jnp.exp(line(2) + line(3) + line(4))
        state = fade * state + got_ref[b, 0:SLOTS, :].astype(F32)
        norm = fade * norm + line(0) + line(1)
        return state, norm

    lax.fori_loop(
        0, blocks, step, (jnp.zeros((SLOTS, HD), F32), jnp.zeros((1, HD), F32)), unroll=4
    )


def prior_states(got):
    return pl.pallas_call(
        prior_body, out_shape=jax.ShapeDtypeStruct(got.shape, BF16), compiler_params=pltpu.CompilerParams(vmem_limit_bytes=4 << 20),
        name="prior_states"
    )(got)


def inner_body(q_ref, k_ref, v_ref, decay_ref, w_ref, num_ref, den_ref, wa_ref, wb_ref, held, sems):
    parting = Parting(w_ref, (wa_ref, wb_ref), held, sems)
    heads, length = decay_ref.shape
    cum = running_sum(padded_decay(decay_ref))
    cum_col = cum.T
    tile = 128
    lane = lax.broadcasted_iota(jnp.int32, (tile, HD), 1)
    for t in range(length // tile):
        rows = slice(t * tile, (t + 1) * tile)
        seen = (t + 1) * tile
        col = lax.broadcasted_iota(jnp.int32, (tile, seen), 1)
        at = lax.broadcasted_iota(jnp.int32, (tile, seen), 0) + t * tile
        causal = col <= at
        if t == 1:
            parting.turn()
        dens = jnp.zeros((tile, HD), F32)
        for h in range(heads):
            cols = slice(h * HD, (h + 1) * HD)
            scores = lax.dot_general(
                feature(q_ref[rows, cols]),
                feature(k_ref[0:seen, cols]),
                (((1,), (1,)), ((), ())),
                preferred_element_type=F32,
            )
            spread = cum_col[rows, h : h + 1] - cum[h : h + 1, 0:seen]
            weights = jnp.where(causal, scores * jnp.exp(jnp.where(causal, spread, 0.0)), 0.0)
            dens = jnp.where(lane == h, jnp.sum(weights, axis=1, keepdims=True), dens)
            num_ref[rows, cols] = jnp.dot(
                weights.astype(BF16), v_ref[0:seen, cols], preferred_element_type=F32
            )
        den_ref[rows, :] = dens
    parting.finish()


def inner_attention(queries, keys, values, decay, both):
    length, width = queries.shape
    return pl.pallas_call(
        inner_body,
        out_shape=[
            jax.ShapeDtypeStruct((length, width), F32),
            jax.ShapeDtypeStruct((length, HD), F32),
            *parts_of(both),
        ],
        in_specs=[ON_CHIP] * 4 + [ANYWHERE],
        out_specs=[ON_CHIP, ON_CHIP, ANYWHERE, ANYWHERE],
        scratch_shapes=parting_scratch(both),
        cost_estimate=pl.CostEstimate(
            flops=4 * length * length * width,
            bytes_accessed=8 * length * width,
            transcendentals=4 * length * length,
        ),
        compiler_params=pltpu.CompilerParams(vmem_limit_bytes=GRANT),
        name="inner_attention",
    )(queries, keys, values, decay, both)


def outer_body(q_ref, decay_ref, prior_ref, num_ref, den_ref, out_ref):
    heads, length = decay_ref.shape
    groups = out_ref.shape[0]
    parts = prior_ref.shape[0] // heads
    damp = jnp.exp(running_sum(padded_decay(decay_ref))).T
    row = lax.broadcasted_iota(jnp.int32, (EXTRA, HD), 0)
    for h in range(heads):
        cols = slice(h * HD, (h + 1) * HD)
        feat = feature(q_ref[:, cols])
        state = prior_ref[h * parts : (h + 1) * parts, 0:SLOTS, :].reshape(HD, HD)
        extra = prior_ref[h * parts, SLOTS:, :].astype(F32)
        norm = jnp.sum(jnp.where(row < 2, extra, 0.0), axis=0, keepdims=True)
        scale = damp[:, h : h + 1]
        num = num_ref[:, cols] + scale * jnp.dot(feat, state, preferred_element_type=F32)
        den = den_ref[:, h : h + 1] + scale * jnp.sum(
            feat.astype(F32) * norm, axis=1, keepdims=True
        )
        out_ref[:, :, cols] = (num / den).astype(BF16).reshape(groups, length // groups, HD)


def outer_attention(queries, decay, prior, num, den, groups):
    length, width = queries.shape
    return pl.pallas_call(
        outer_body,
        out_shape=jax.ShapeDtypeStruct((groups, length // groups, width), BF16),
        compiler_params=pltpu.CompilerParams(vmem_limit_bytes=50 << 20),
        name="outer_attention",
    )(queries, decay, prior, num, den)


def route_body(ids_ref, gates_ref, w_ref, *refs):
    dispatch_ref, combine_ref, even_ref, odd_ref, wa_ref, wb_ref, held, sems = refs
    parting = Parting(w_ref, (wa_ref, wb_ref), held, sems)
    rows = ids_ref.shape[1]
    expert = lax.broadcasted_iota(jnp.int32, (E, rows), 0)
    hits = jnp.zeros((E, rows), F32)
    gates = jnp.zeros((E, rows), F32)
    for k in range(TOPK):
        match = expert == ids_ref[k : k + 1, :]
        hits = jnp.where(match, 1.0, hits)
        gates = jnp.where(match, gates_ref[k : k + 1, :], gates)
    before = (
        lax.broadcasted_iota(jnp.int32, (rows, rows), 0)
        < lax.broadcasted_iota(jnp.int32, (rows, rows), 1)
    ).astype(BF16)
    slot = jnp.dot(hits.astype(BF16), before, preferred_element_type=F32)
    slot = jnp.where(hits > 0.0, slot, -1.0)
    gates = gates.astype(BF16).astype(F32)
    half = SLOTS // CHUNKS
    parting.turn()
    for chunk in range(CHUNKS):
        place = lax.broadcasted_iota(jnp.int32, (E, half, rows), 1) + chunk * half
        here = jnp.broadcast_to(slot[:, None, :], (E, half, rows)) == place.astype(F32)
        dispatch_ref[chunk] = jnp.where(here, 1.0, 0.0).reshape(E * half, rows).astype(BF16)
        mix = jnp.where(here, jnp.broadcast_to(gates[:, None, :], (E, half, rows)), 0.0)
        combine_ref[chunk] = mix.reshape(E * half, rows).astype(BF16)
        if chunk == 0:
            by_parity = mix.reshape(E // 2, 2, half, rows)
            for parity, ref in ((0, even_ref), (1, odd_ref)):
                ref[...] = by_parity[:, parity].reshape(E // 2 * half, rows).astype(BF16)
    parting.finish()


def route(ids, gates, both):
    rows = ids.shape[1]
    shape = jax.ShapeDtypeStruct((CHUNKS, E * SLOTS // CHUNKS, rows), BF16)
    part = jax.ShapeDtypeStruct((E // 2 * SLOTS // CHUNKS, rows), BF16)
    return pl.pallas_call(
        route_body,
        out_shape=[shape, shape, part, part, *parts_of(both)],
        in_specs=[ON_CHIP, ON_CHIP, ANYWHERE],
        out_specs=[ON_CHIP] * 4 + [ANYWHERE] * 2,
        scratch_shapes=parting_scratch(both), compiler_params=pltpu.CompilerParams(vmem_limit_bytes=GRANT),
        name="route",
    )(ids, gates, both)


NT = (((1,), (1,)), ((), ()))
TN = (((0,), (0,)), ((), ()))


def expert_rows(x, weights, e, ready, emit):
    ready(0)
    gate = lax.dot_general(weights[e, 0], x, NT, preferred_element_type=F32)
    ready(1)
    up = lax.dot_general(weights[e, 1], x, NT, preferred_element_type=F32)
    hidden = (jax.nn.silu(gate) * up).astype(BF16)
    ready(2)
    width = D // 4

    def down(i, inner):
        cols = pl.ds(pl.multiple_of(i * width, width), width)
        part = lax.dot_general(hidden, weights[e, 2, :, cols], TN, preferred_element_type=F32)
        emit(cols, part.astype(BF16))
        return inner

    lax.fori_loop(0, 4, down, 0)


def experts_body(sets, *refs):
    count = 1 + max(at for pair in sets for at, _ in pair)
    rows_in = refs[:count]
    own = refs[count : count + 3]
    fars = (refs[count + 3 : count + 6], refs[count + 6 : count + 9])
    outs = refs[count + 9 : count + 9 + len(sets)]
    ws, xs, sems = refs[-3:]
    quarter = fars[0][0].shape[0]
    _, n_sets, blocks, rows, _ = xs.shape
    for e in range(2):
        for j, pair in enumerate(sets):
            at, first = pair[e]
            source = rows_in[at].at[:, first : first + rows, :]
            pltpu.make_async_copy(source, xs.at[e, j], sems.at[e, 6 + j]).start()
        for i in range(3):
            low = ws.at[e, i, 0:quarter]
            high = ws.at[e, i, quarter : 2 * quarter]
            pltpu.make_async_copy(own[i].at[e], low, sems.at[e, 2 * i]).start()
            pltpu.make_async_copy(fars[e][i], high, sems.at[e, 2 * i + 1]).start()

    def expert(e, carry):
        def ready(i):
            for part in range(2):
                held = ws.at[e, i, part * quarter : (part + 1) * quarter]
                pltpu.make_async_copy(fars[0][0], held, sems.at[e, 2 * i + part]).wait()

        def emit(cols, part):
            at = pl.ds(pl.multiple_of(e * rows, rows), rows)
            part = part.reshape(n_sets, blocks, rows, part.shape[1])
            for j in range(n_sets):
                outs[j][:, at, cols] = part[j]

        for j in range(n_sets):
            pltpu.make_async_copy(
                rows_in[0].at[:, 0:rows, :], xs.at[e, j], sems.at[e, 6 + j]
            ).wait()
        expert_rows(xs[e].reshape(-1, D), ws, e, ready, emit)
        return carry

    lax.fori_loop(0, 2, expert, 0)


def expert_cost(total, quarter, loaded):
    return pl.CostEstimate(
        flops=12 * total * quarter * D,
        bytes_accessed=loaded * 24 * quarter * D + 4 * total * D,
        transcendentals=2 * total * quarter,
    )


def experts(xs, sets, own, fars, keep=False):
    quarter = fars[0][0].shape[0]
    blocks = xs[0].shape[0]
    rows = SLOTS // CHUNKS
    out_shape = [jax.ShapeDtypeStruct((blocks, 2 * rows, D), BF16)] * len(sets)
    anywhere = pl.BlockSpec(memory_space=pl.ANY)
    held = pltpu.VMEM((2, 3, 2 * quarter, D), BF16)
    scratch = [
        pltpu.VMEM((2, len(sets), blocks, rows, D), BF16),
        pltpu.SemaphoreType.DMA((2, 6 + len(sets))),
    ]
    return pl.pallas_call(
        functools.partial(experts_body, sets),
        out_shape=out_shape + [held] if keep else out_shape,
        in_specs=[anywhere] * (len(xs) + 9),
        scratch_shapes=scratch if keep else [held] + scratch,
        compiler_params=pltpu.CompilerParams(vmem_limit_bytes=KEEP_GRANT if keep else GRANT),
        cost_estimate=expert_cost(2 * blocks * rows * len(sets), quarter, 1),
        name="experts",
    )(*xs, *own, *fars[0], *fars[1])


def last_body(xa, xb, weights, out_a, out_b):
    for e, (x_ref, out) in enumerate(((xa, out_a), (xb, out_b))):

        def emit(cols, part, out=out):
            out[:, cols] = part

        expert_rows(x_ref[...].reshape(-1, D), weights, e, lambda i: None, emit)


def last_experts(xa, xb, weights):
    blocks, rows, _ = xa.shape
    return pl.pallas_call(
        last_body,
        out_shape=[jax.ShapeDtypeStruct((blocks * rows, D), BF16)] * 2,
        compiler_params=pltpu.CompilerParams(vmem_limit_bytes=KEEP_GRANT),
        cost_estimate=expert_cost(2 * blocks * rows, weights.shape[2] // 2, 0),
        name="last_experts",
    )(xa, xb, weights)


def merge_body(own, came_a, came_b, out):
    blocks, rows, _ = out.shape
    rows = rows // 2
    for at, came in ((0, came_a), (rows, came_b)):
        back = came[...].astype(F32).reshape(blocks, rows, D)
        out[:, at : at + rows, :] = (own[:, at : at + rows, :].astype(F32) + back).astype(BF16)


def merge(own, came_a, came_b):
    blocks, rows, _ = own.shape
    steps = 4
    wide = pl.BlockSpec((blocks // steps, rows, D), lambda i: (i, 0, 0))
    flat = pl.BlockSpec((came_a.shape[0] // steps, D), lambda i: (i, 0))
    return pl.pallas_call(
        merge_body,
        grid=(steps,),
        out_shape=jax.ShapeDtypeStruct(own.shape, BF16),
        in_specs=[wide, flat, flat],
        out_specs=wide,
        compiler_params=pltpu.CompilerParams(vmem_limit_bytes=16 << 20),
        cost_estimate=pl.CostEstimate(
            flops=blocks * rows * D, bytes_accessed=6 * blocks * rows * D, transcendentals=0
        ),
        name="merge",
    )(own, came_a, came_b)


def partner_body(back, mix_a, mix_b, far_ref, near_ref):
    blocks, rows, width = back.shape
    rows = rows // 2
    for at, mix, out in ((0, mix_a, far_ref), (rows, mix_b, near_ref)):
        part = back[:, at : at + rows, :].reshape(blocks * rows, width)
        out[...] = lax.dot_general(
            mix[...], part, (((0,), (0,)), ((), ())), preferred_element_type=F32
        ).astype(BF16)


def partner_mix(back, mix_a, mix_b):
    blocks, rows, _ = back.shape
    tokens = mix_a.shape[1]
    steps = 4
    out = jax.ShapeDtypeStruct((tokens, D), BF16)
    whole = pl.BlockSpec(mix_a.shape, lambda i: (0, 0))
    strip = pl.BlockSpec((tokens, D // steps), lambda i: (0, i))
    return pl.pallas_call(
        partner_body,
        grid=(steps,),
        out_shape=[out, out],
        in_specs=[
            pl.BlockSpec((blocks, rows, D // steps), lambda i: (0, 0, i)),
            whole,
            whole,
        ],
        out_specs=[strip, strip],
        compiler_params=pltpu.CompilerParams(vmem_limit_bytes=16 << 20),
        cost_estimate=pl.CostEstimate(
            flops=2 * blocks * rows * tokens * D,
            bytes_accessed=2 * blocks * rows * D,
            transcendentals=0,
        ),
        name="partner_mix",
    )(back, mix_a, mix_b)


def on_device(
    query_heads,
    key_heads,
    value_heads,
    log_decay,
    residual,
    out_weight,
    norm_gain,
    expert_ids,
    gate_weights,
    gate_proj,
    up_proj,
    down_proj,
):
    n_ctx = lax.axis_size("ctx")
    gate_t = jnp.swapaxes(gate_proj, 1, 2)
    up_t = jnp.swapaxes(up_proj, 1, 2)
    pairs = ((NEAR, FAR), (FAR, NEAR))
    own_w = (gate_t, up_t, down_proj)

    def send(parts):
        far = []
        for which in range(2):
            far.append(lax.ppermute(parts[which], "grp", pairs[which][0]))
        return far

    n_grp = lax.axis_size("grp")
    payload, *gates = local_states(key_heads, value_heads, log_decay, n_ctx, gate_t)
    far_gate = send(gates)
    got = lax.all_to_all(payload, "ctx", 0, 0, tiled=True)
    dispatch, combine, even, odd, *downs = route(
        jnp.swapaxes(expert_ids, 0, 1), jnp.swapaxes(gate_weights, 0, 1), down_proj
    )
    far_even = lax.ppermute(even, "grp", FAR)
    near_odd = lax.ppermute(odd, "grp", NEAR)
    back = prior_states(got)
    prior = lax.all_to_all(back, "ctx", 0, 0, tiled=True)
    num, den, *ups = inner_attention(
        query_heads, key_heads, value_heads, log_decay, up_t
    )
    mixed = outer_attention(query_heads, log_decay, prior, num, den, n_grp)
    far_w = list(zip(far_gate, send(ups), send(downs)))
    heads_in = lax.all_to_all(mixed, "grp", 0, 0, tiled=True)
    projected = jnp.einsum(
        "gtc,gcd->td", heads_in, out_weight.reshape(n_grp, -1, D), preferred_element_type=F32
    )
    attended = (residual.astype(F32) + projected).astype(BF16)
    widened = attended.astype(F32)
    normed = (
        widened * lax.rsqrt(jnp.mean(widened * widened, axis=1, keepdims=True) + 1e-06) * norm_gain
    ).astype(BF16)

    half = SLOTS // CHUNKS
    sent = []
    for chunk in range(CHUNKS):
        buffer = jnp.dot(dispatch[chunk], normed, preferred_element_type=F32).astype(BF16)
        sent.append(
            lax.all_to_all(buffer.reshape(n_ctx, 2 * half, D), "ctx", 0, 0, tiled=True)
        )
    others = []
    for chunk in range(CHUNKS):
        for which in range(2):
            own = sent[chunk][:, which * half : (which + 1) * half]
            others.append(lax.ppermute(own, "grp", pairs[which][1]))

    def home(rows):
        return lax.all_to_all(rows, "ctx", 0, 0, tiled=True)

    def mix(chunk, back):
        return lax.dot_general(
            combine[chunk],
            back.reshape(-1, D),
            (((0,), (0,)), ((), ())),
            preferred_element_type=F32,
        )

    (own0,) = experts((sent[0],), (((0, 0), (0, half)),), own_w, far_w)
    back_own0 = home(own0)
    own1, other0, held = experts(
        (sent[1], others[0], others[1]),
        (((0, 0), (0, half)), ((1, 0), (2, 0))),
        own_w,
        far_w,
        keep=True,
    )
    back_other0 = home(other0)
    for_far, for_near = partner_mix(back_other0, far_even, near_odd)
    from_far = lax.ppermute(for_far, "grp", FAR)
    from_near = lax.ppermute(for_near, "grp", NEAR)

    results = last_experts(others[2], others[3], held)
    came = []
    for which in range(2):
        came.append(lax.ppermute(results[which], "grp", pairs[which][1]))
    back1 = home(merge(own1, *came))
    so_far = lax.optimization_barrier(widened + mix(0, back_own0))
    total = so_far + from_far.astype(F32) + from_near.astype(F32) + mix(1, back1)
    return (attended, total.astype(BF16))


def solution(mesh):
    placed = (
        P("ctx", "grp"),
        P("ctx", "grp"),
        P("ctx", "grp"),
        P("grp", "ctx"),
        P(("ctx", "grp"), None),
        P(),
        P(),
        P(("ctx", "grp"), None),
        P(("ctx", "grp"), None),
        P("ctx", None, "grp"),
        P("ctx", None, "grp"),
        P("ctx", "grp", None),
    )

    return jax.shard_map(
        on_device,
        mesh=mesh,
        in_specs=placed,
        out_specs=(P(("ctx", "grp"), None), P(("ctx", "grp"), None)),
        check_vma=False,
    )
```

```python
import functools

import jax
import jax.numpy as jnp
from jax import lax
from jax.experimental import pallas as pl
from jax.experimental.pallas import tpu as pltpu
from jax.sharding import PartitionSpec as P


D = 2048
HD = 128
E = 64
TOPK = 6
SLOTS = 16
CHUNKS = 2
EXTRA = 8
GRANT = 58 << 20
KEEP_GRANT = 16 << 20
MIDDLE_GRANT = 36 << 20
FAR = [(0, 3), (3, 0), (1, 2), (2, 1)]
NEAR = [(0, 1), (1, 0), (2, 3), (3, 2)]
F32 = jnp.float32
BF16 = jnp.bfloat16
ANYWHERE = pl.BlockSpec(memory_space=pl.ANY)
ON_CHIP = pl.BlockSpec(memory_space=pltpu.VMEM)


def feature(values):
    wide = values.astype(F32)
    return jnp.where(wide > 0, wide + 1.0, jnp.exp(jnp.minimum(wide, 0.0))).astype(BF16)


def running_sum(rows):
    lanes = lax.broadcasted_iota(jnp.int32, rows.shape, 1)
    step = 1
    while step < rows.shape[1]:
        rows = rows + jnp.where(lanes >= step, pltpu.roll(rows, step, 1), 0.0)
        step *= 2
    return rows


def padded_decay(decay_ref):
    decay = decay_ref[...]
    return jnp.concatenate([decay, jnp.zeros((8 - decay.shape[0], decay.shape[1]), F32)], axis=0)


class Parting:
    def __init__(self, both, parts, held, sems):
        self.load = pltpu.make_async_copy(both, held, sems.at[0])
        self.stores = [
            pltpu.make_async_copy(held.at[e], parts[e], sems.at[1 + e]) for e in range(2)
        ]
        self.load.start()

    def turn(self):
        self.load.wait()
        for store in self.stores:
            store.start()

    def finish(self):
        for store in self.stores:
            store.wait()


def parting_scratch(both):
    return [pltpu.VMEM(both.shape, BF16), pltpu.SemaphoreType.DMA((3,))]


def parts_of(both):
    return [jax.ShapeDtypeStruct(both.shape[1:], BF16)] * 2


def state_body(k_ref, v_ref, decay_ref, w_ref, out_ref, wa_ref, wb_ref, held, sems):
    parting = Parting(w_ref, (wa_ref, wb_ref), held, sems)
    heads, length = decay_ref.shape
    cum = running_sum(padded_decay(decay_ref))
    total = cum[:, length - 1 :]
    fade = jnp.exp(total - cum).T
    parts = out_ref.shape[0] // heads
    parting.turn()
    row = lax.broadcasted_iota(jnp.int32, (EXTRA, HD), 0)
    for h in range(heads):
        cols = slice(h * HD, (h + 1) * HD)
        tail = feature(k_ref[:, cols]).astype(F32) * fade[:, h : h + 1]
        norm = jnp.sum(tail, axis=0, keepdims=True)
        state = lax.dot_general(
            tail.astype(BF16), v_ref[:, cols], (((0,), (0,)), ((), ())), preferred_element_type=F32
        )
        out_ref[h * parts : (h + 1) * parts, 0:SLOTS, :] = state.astype(BF16).reshape(
            parts, SLOTS, HD
        )
        norm_hi = norm.astype(BF16).astype(F32)
        tot = jnp.broadcast_to(total[h : h + 1, :], (1, HD))
        tot_hi = tot.astype(BF16).astype(F32)
        tot_lo = (tot - tot_hi).astype(BF16).astype(F32)
        extra = jnp.zeros((EXTRA, HD), F32)
        for i, line in enumerate((norm_hi, norm - norm_hi, tot_hi, tot_lo, tot - tot_hi - tot_lo)):
            extra = jnp.where(row == i, line, extra)
        out_ref[h * parts : (h + 1) * parts, SLOTS:, :] = jnp.broadcast_to(
            extra.astype(BF16)[None], (parts, EXTRA, HD)
        )
    parting.finish()


def local_states(keys, values, decay, blocks, both):
    return pl.pallas_call(
        state_body,
        out_shape=[jax.ShapeDtypeStruct((blocks, SLOTS + EXTRA, HD), BF16), *parts_of(both)],
        in_specs=[ON_CHIP] * 3 + [ANYWHERE],
        out_specs=[ON_CHIP, ANYWHERE, ANYWHERE],
        scratch_shapes=parting_scratch(both),
        compiler_params=pltpu.CompilerParams(vmem_limit_bytes=GRANT),
        name="local_states",
    )(keys, values, decay, both)


def prior_body(got_ref, out_ref):
    blocks = got_ref.shape[0]
    row = lax.broadcasted_iota(jnp.int32, (EXTRA, HD), 0)

    def step(b, carry):
        state, norm = carry
        extra = got_ref[b, SLOTS:, :].astype(F32)

        def line(i):
            return jnp.sum(jnp.where(row == i, extra, 0.0), axis=0, keepdims=True)

        norm_hi = norm.astype(BF16).astype(F32)
        out_ref[b, 0:SLOTS, :] = state.astype(BF16)
        out_ref[b, SLOTS:, :] = jnp.where(
            row == 0, norm_hi, jnp.where(row == 1, norm - norm_hi, 0.0)
        ).astype(BF16)
        fade = jnp.exp(line(2) + line(3) + line(4))
        state = fade * state + got_ref[b, 0:SLOTS, :].astype(F32)
        norm = fade * norm + line(0) + line(1)
        return state, norm

    lax.fori_loop(
        0, blocks, step, (jnp.zeros((SLOTS, HD), F32), jnp.zeros((1, HD), F32)), unroll=4
    )


def prior_states(got):
    return pl.pallas_call(
        prior_body, out_shape=jax.ShapeDtypeStruct(got.shape, BF16), compiler_params=pltpu.CompilerParams(vmem_limit_bytes=4 << 20),
        name="prior_states"
    )(got)


def inner_body(q_ref, k_ref, v_ref, decay_ref, w_ref, num_ref, den_ref, wa_ref, wb_ref, held, sems):
    parting = Parting(w_ref, (wa_ref, wb_ref), held, sems)
    heads, length = decay_ref.shape
    cum = running_sum(padded_decay(decay_ref))
    cum_col = cum.T
    tile = 128
    lane = lax.broadcasted_iota(jnp.int32, (tile, HD), 1)
    for t in range(length // tile):
        rows = slice(t * tile, (t + 1) * tile)
        seen = (t + 1) * tile
        col = lax.broadcasted_iota(jnp.int32, (tile, seen), 1)
        at = lax.broadcasted_iota(jnp.int32, (tile, seen), 0) + t * tile
        causal = col <= at
        if t == 1:
            parting.turn()
        dens = jnp.zeros((tile, HD), F32)
        for h in range(heads):
            cols = slice(h * HD, (h + 1) * HD)
            scores = lax.dot_general(
                feature(q_ref[rows, cols]),
                feature(k_ref[0:seen, cols]),
                (((1,), (1,)), ((), ())),
                preferred_element_type=F32,
            )
            spread = cum_col[rows, h : h + 1] - cum[h : h + 1, 0:seen]
            weights = jnp.where(causal, scores * jnp.exp(jnp.where(causal, spread, 0.0)), 0.0)
            dens = jnp.where(lane == h, jnp.sum(weights, axis=1, keepdims=True), dens)
            num_ref[rows, cols] = jnp.dot(
                weights.astype(BF16), v_ref[0:seen, cols], preferred_element_type=F32
            )
        den_ref[rows, :] = dens
    parting.finish()


def inner_attention(queries, keys, values, decay, both):
    length, width = queries.shape
    return pl.pallas_call(
        inner_body,
        out_shape=[
            jax.ShapeDtypeStruct((length, width), F32),
            jax.ShapeDtypeStruct((length, HD), F32),
            *parts_of(both),
        ],
        in_specs=[ON_CHIP] * 4 + [ANYWHERE],
        out_specs=[ON_CHIP, ON_CHIP, ANYWHERE, ANYWHERE],
        scratch_shapes=parting_scratch(both),
        cost_estimate=pl.CostEstimate(
            flops=4 * length * length * width,
            bytes_accessed=8 * length * width,
            transcendentals=4 * length * length,
        ),
        compiler_params=pltpu.CompilerParams(vmem_limit_bytes=GRANT),
        name="inner_attention",
    )(queries, keys, values, decay, both)


def outer_body(q_ref, decay_ref, prior_ref, num_ref, den_ref, out_ref):
    heads, length = decay_ref.shape
    groups = out_ref.shape[0]
    parts = prior_ref.shape[0] // heads
    damp = jnp.exp(running_sum(padded_decay(decay_ref))).T
    row = lax.broadcasted_iota(jnp.int32, (EXTRA, HD), 0)
    for h in range(heads):
        cols = slice(h * HD, (h + 1) * HD)
        feat = feature(q_ref[:, cols])
        state = prior_ref[h * parts : (h + 1) * parts, 0:SLOTS, :].reshape(HD, HD)
        extra = prior_ref[h * parts, SLOTS:, :].astype(F32)
        norm = jnp.sum(jnp.where(row < 2, extra, 0.0), axis=0, keepdims=True)
        scale = damp[:, h : h + 1]
        num = num_ref[:, cols] + scale * jnp.dot(feat, state, preferred_element_type=F32)
        den = den_ref[:, h : h + 1] + scale * jnp.sum(
            feat.astype(F32) * norm, axis=1, keepdims=True
        )
        out_ref[:, :, cols] = (num / den).astype(BF16).reshape(groups, length // groups, HD)


def outer_attention(queries, decay, prior, num, den, groups):
    length, width = queries.shape
    return pl.pallas_call(
        outer_body,
        out_shape=jax.ShapeDtypeStruct((groups, length // groups, width), BF16),
        compiler_params=pltpu.CompilerParams(vmem_limit_bytes=50 << 20),
        name="outer_attention",
    )(queries, decay, prior, num, den)


def route_body(ids_ref, gates_ref, w_ref, *refs):
    dispatch_ref, combine_ref, even_ref, odd_ref, wa_ref, wb_ref, held, sems = refs
    parting = Parting(w_ref, (wa_ref, wb_ref), held, sems)
    rows = ids_ref.shape[1]
    expert = lax.broadcasted_iota(jnp.int32, (E, rows), 0)
    hits = jnp.zeros((E, rows), F32)
    gates = jnp.zeros((E, rows), F32)
    for k in range(TOPK):
        match = expert == ids_ref[k : k + 1, :]
        hits = jnp.where(match, 1.0, hits)
        gates = jnp.where(match, gates_ref[k : k + 1, :], gates)
    before = (
        lax.broadcasted_iota(jnp.int32, (rows, rows), 0)
        < lax.broadcasted_iota(jnp.int32, (rows, rows), 1)
    ).astype(BF16)
    slot = jnp.dot(hits.astype(BF16), before, preferred_element_type=F32)
    slot = jnp.where(hits > 0.0, slot, -1.0)
    gates = gates.astype(BF16).astype(F32)
    half = SLOTS // CHUNKS
    parting.turn()
    for chunk in range(CHUNKS):
        place = lax.broadcasted_iota(jnp.int32, (E, half, rows), 1) + chunk * half
        here = jnp.broadcast_to(slot[:, None, :], (E, half, rows)) == place.astype(F32)
        dispatch_ref[chunk] = jnp.where(here, 1.0, 0.0).reshape(E * half, rows).astype(BF16)
        mix = jnp.where(here, jnp.broadcast_to(gates[:, None, :], (E, half, rows)), 0.0)
        combine_ref[chunk] = mix.reshape(E * half, rows).astype(BF16)
        if chunk == 0:
            by_parity = mix.reshape(E // 2, 2, half, rows)
            for parity, ref in ((0, even_ref), (1, odd_ref)):
                ref[...] = by_parity[:, parity].reshape(E // 2 * half, rows).astype(BF16)
    parting.finish()


def route(ids, gates, both):
    rows = ids.shape[1]
    shape = jax.ShapeDtypeStruct((CHUNKS, E * SLOTS // CHUNKS, rows), BF16)
    part = jax.ShapeDtypeStruct((E // 2 * SLOTS // CHUNKS, rows), BF16)
    return pl.pallas_call(
        route_body,
        out_shape=[shape, shape, part, part, *parts_of(both)],
        in_specs=[ON_CHIP, ON_CHIP, ANYWHERE],
        out_specs=[ON_CHIP] * 4 + [ANYWHERE] * 2,
        scratch_shapes=parting_scratch(both), compiler_params=pltpu.CompilerParams(vmem_limit_bytes=GRANT),
        name="route",
    )(ids, gates, both)


NT = (((1,), (1,)), ((), ()))
TN = (((0,), (0,)), ((), ()))


def expert_rows(x, weights, e, ready, emit):
    ready(0)
    gate = lax.dot_general(weights[e, 0], x, NT, preferred_element_type=F32)
    ready(1)
    up = lax.dot_general(weights[e, 1], x, NT, preferred_element_type=F32)
    hidden = (jax.nn.silu(gate) * up).astype(BF16)
    ready(2)
    width = D // 4

    def down(i, inner):
        cols = pl.ds(pl.multiple_of(i * width, width), width)
        part = lax.dot_general(hidden, weights[e, 2, :, cols], TN, preferred_element_type=F32)
        emit(cols, part.astype(BF16))
        return inner

    lax.fori_loop(0, 4, down, 0)


def experts_body(sets, *refs):
    count = 1 + max(at for pair in sets for at, _ in pair)
    rows_in = refs[:count]
    own = refs[count : count + 3]
    fars = (refs[count + 3 : count + 6], refs[count + 6 : count + 9])
    outs = refs[count + 9 : count + 9 + len(sets)]
    ws, xs, sems = refs[-3:]
    quarter = fars[0][0].shape[0]
    _, n_sets, blocks, rows, _ = xs.shape
    for e in range(2):
        for j, pair in enumerate(sets):
            at, first = pair[e]
            source = rows_in[at].at[:, first : first + rows, :]
            pltpu.make_async_copy(source, xs.at[e, j], sems.at[e, 6 + j]).start()
        for i in range(3):
            low = ws.at[e, i, 0:quarter]
            high = ws.at[e, i, quarter : 2 * quarter]
            pltpu.make_async_copy(own[i].at[e], low, sems.at[e, 2 * i]).start()
            pltpu.make_async_copy(fars[e][i], high, sems.at[e, 2 * i + 1]).start()

    def expert(e, carry):
        def ready(i):
            for part in range(2):
                held = ws.at[e, i, part * quarter : (part + 1) * quarter]
                pltpu.make_async_copy(fars[0][0], held, sems.at[e, 2 * i + part]).wait()

        def emit(cols, part):
            at = pl.ds(pl.multiple_of(e * rows, rows), rows)
            part = part.reshape(n_sets, blocks, rows, part.shape[1])
            for j in range(n_sets):
                outs[j][:, at, cols] = part[j]

        for j in range(n_sets):
            pltpu.make_async_copy(
                rows_in[0].at[:, 0:rows, :], xs.at[e, j], sems.at[e, 6 + j]
            ).wait()
        expert_rows(xs[e].reshape(-1, D), ws, e, ready, emit)
        return carry

    lax.fori_loop(0, 2, expert, 0)


def expert_cost(total, quarter, loaded):
    return pl.CostEstimate(
        flops=12 * total * quarter * D,
        bytes_accessed=loaded * 24 * quarter * D + 4 * total * D,
        transcendentals=2 * total * quarter,
    )


def experts(xs, sets, own, fars, keep=False):
    quarter = fars[0][0].shape[0]
    blocks = xs[0].shape[0]
    rows = SLOTS // CHUNKS
    out_shape = [jax.ShapeDtypeStruct((blocks, 2 * rows, D), BF16)] * len(sets)
    anywhere = pl.BlockSpec(memory_space=pl.ANY)
    held = pltpu.VMEM((2, 3, 2 * quarter, D), BF16)
    scratch = [
        pltpu.VMEM((2, len(sets), blocks, rows, D), BF16),
        pltpu.SemaphoreType.DMA((2, 6 + len(sets))),
    ]
    return pl.pallas_call(
        functools.partial(experts_body, sets),
        out_shape=out_shape + [held] if keep else out_shape,
        in_specs=[anywhere] * (len(xs) + 9),
        scratch_shapes=scratch if keep else [held] + scratch,
        compiler_params=pltpu.CompilerParams(vmem_limit_bytes=MIDDLE_GRANT if keep else GRANT),
        cost_estimate=expert_cost(2 * blocks * rows * len(sets), quarter, 1),
        name="experts",
    )(*xs, *own, *fars[0], *fars[1])


def last_body(xa, xb, weights, out_a, out_b, xs, ys, sems):
    loads, stores = [], []
    for e, (x_ref, out) in enumerate(((xa, out_a), (xb, out_b))):
        loads.append(pltpu.make_async_copy(x_ref, xs.at[e], sems.at[e]))
        stores.append(pltpu.make_async_copy(ys.at[e], out, sems.at[2 + e]))
        loads[e].start()
    for e in range(2):

        def emit(cols, part, e=e):
            ys[e, :, cols] = part

        loads[e].wait()
        expert_rows(xs[e].reshape(-1, D), weights, e, lambda i: None, emit)
        stores[e].start()
    for store in stores:
        store.wait()


def last_experts(xa, xb, weights):
    blocks, rows, _ = xa.shape
    total = blocks * rows
    return pl.pallas_call(
        last_body,
        out_shape=[jax.ShapeDtypeStruct((total, D), BF16)] * 2,
        in_specs=[ANYWHERE, ANYWHERE, ON_CHIP],
        out_specs=[ANYWHERE, ANYWHERE],
        scratch_shapes=[
            pltpu.VMEM((2, blocks, rows, D), BF16),
            pltpu.VMEM((2, total, D), BF16),
            pltpu.SemaphoreType.DMA((4,)),
        ],
        compiler_params=pltpu.CompilerParams(vmem_limit_bytes=KEEP_GRANT),
        cost_estimate=expert_cost(2 * total, weights.shape[2] // 2, 0),
        name="last_experts",
    )(xa, xb, weights)


def merge_body(own, came_a, came_b, out):
    blocks, rows, _ = out.shape
    rows = rows // 2
    for at, came in ((0, came_a), (rows, came_b)):
        back = came[...].astype(F32).reshape(blocks, rows, D)
        out[:, at : at + rows, :] = (own[:, at : at + rows, :].astype(F32) + back).astype(BF16)


def merge(own, came_a, came_b):
    blocks, rows, _ = own.shape
    steps = 4
    wide = pl.BlockSpec((blocks // steps, rows, D), lambda i: (i, 0, 0))
    flat = pl.BlockSpec((came_a.shape[0] // steps, D), lambda i: (i, 0))
    return pl.pallas_call(
        merge_body,
        grid=(steps,),
        out_shape=jax.ShapeDtypeStruct(own.shape, BF16),
        in_specs=[wide, flat, flat],
        out_specs=wide,
        compiler_params=pltpu.CompilerParams(vmem_limit_bytes=16 << 20),
        cost_estimate=pl.CostEstimate(
            flops=blocks * rows * D, bytes_accessed=6 * blocks * rows * D, transcendentals=0
        ),
        name="merge",
    )(own, came_a, came_b)


def partner_body(back, mix_a, mix_b, far_ref, near_ref):
    blocks, rows, width = back.shape
    rows = rows // 2
    for at, mix, out in ((0, mix_a, far_ref), (rows, mix_b, near_ref)):
        part = back[:, at : at + rows, :].reshape(blocks * rows, width)
        out[...] = lax.dot_general(
            mix[...], part, (((0,), (0,)), ((), ())), preferred_element_type=F32
        ).astype(BF16)


def partner_mix(back, mix_a, mix_b):
    blocks, rows, _ = back.shape
    tokens = mix_a.shape[1]
    steps = 4
    out = jax.ShapeDtypeStruct((tokens, D), BF16)
    whole = pl.BlockSpec(mix_a.shape, lambda i: (0, 0))
    strip = pl.BlockSpec((tokens, D // steps), lambda i: (0, i))
    return pl.pallas_call(
        partner_body,
        grid=(steps,),
        out_shape=[out, out],
        in_specs=[
            pl.BlockSpec((blocks, rows, D // steps), lambda i: (0, 0, i)),
            whole,
            whole,
        ],
        out_specs=[strip, strip],
        compiler_params=pltpu.CompilerParams(vmem_limit_bytes=16 << 20),
        cost_estimate=pl.CostEstimate(
            flops=2 * blocks * rows * tokens * D,
            bytes_accessed=2 * blocks * rows * D,
            transcendentals=0,
        ),
        name="partner_mix",
    )(back, mix_a, mix_b)


def on_device(
    query_heads,
    key_heads,
    value_heads,
    log_decay,
    residual,
    out_weight,
    norm_gain,
    expert_ids,
    gate_weights,
    gate_proj,
    up_proj,
    down_proj,
):
    n_ctx = lax.axis_size("ctx")
    gate_t = jnp.swapaxes(gate_proj, 1, 2)
    up_t = jnp.swapaxes(up_proj, 1, 2)
    pairs = ((NEAR, FAR), (FAR, NEAR))
    own_w = (gate_t, up_t, down_proj)

    def send(parts):
        far = []
        for which in range(2):
            far.append(lax.ppermute(parts[which], "grp", pairs[which][0]))
        return far

    n_grp = lax.axis_size("grp")
    payload, *gates = local_states(key_heads, value_heads, log_decay, n_ctx, gate_t)
    far_gate = send(gates)
    got = lax.all_to_all(payload, "ctx", 0, 0, tiled=True)
    dispatch, combine, even, odd, *downs = route(
        jnp.swapaxes(expert_ids, 0, 1), jnp.swapaxes(gate_weights, 0, 1), down_proj
    )
    far_even = lax.ppermute(even, "grp", FAR)
    near_odd = lax.ppermute(odd, "grp", NEAR)
    back = prior_states(got)
    prior = lax.all_to_all(back, "ctx", 0, 0, tiled=True)
    num, den, *ups = inner_attention(
        query_heads, key_heads, value_heads, log_decay, up_t
    )
    mixed = outer_attention(query_heads, log_decay, prior, num, den, n_grp)
    far_w = list(zip(far_gate, send(ups), send(downs)))
    heads_in = lax.all_to_all(mixed, "grp", 0, 0, tiled=True)
    projected = jnp.einsum(
        "gtc,gcd->td", heads_in, out_weight.reshape(n_grp, -1, D), preferred_element_type=F32
    )
    attended = (residual.astype(F32) + projected).astype(BF16)
    widened = attended.astype(F32)
    normed = (
        widened * lax.rsqrt(jnp.mean(widened * widened, axis=1, keepdims=True) + 1e-06) * norm_gain
    ).astype(BF16)

    half = SLOTS // CHUNKS
    sent = []
    for chunk in range(CHUNKS):
        buffer = jnp.dot(dispatch[chunk], normed, preferred_element_type=F32).astype(BF16)
        sent.append(
            lax.all_to_all(buffer.reshape(n_ctx, 2 * half, D), "ctx", 0, 0, tiled=True)
        )
    others = []
    for chunk in range(CHUNKS):
        for which in range(2):
            own = sent[chunk][:, which * half : (which + 1) * half]
            others.append(lax.ppermute(own, "grp", pairs[which][1]))

    def home(rows):
        return lax.all_to_all(rows, "ctx", 0, 0, tiled=True)

    def mix(chunk, back):
        return lax.dot_general(
            combine[chunk],
            back.reshape(-1, D),
            (((0,), (0,)), ((), ())),
            preferred_element_type=F32,
        )

    (own0,) = experts((sent[0],), (((0, 0), (0, half)),), own_w, far_w)
    back_own0 = home(own0)
    own1, other0, held = experts(
        (sent[1], others[0], others[1]),
        (((0, 0), (0, half)), ((1, 0), (2, 0))),
        own_w,
        far_w,
        keep=True,
    )
    back_other0 = home(other0)
    for_far, for_near = partner_mix(back_other0, far_even, near_odd)
    from_far = lax.ppermute(for_far, "grp", FAR)
    from_near = lax.ppermute(for_near, "grp", NEAR)

    results = last_experts(others[2], others[3], held)
    came = []
    for which in range(2):
        came.append(lax.ppermute(results[which], "grp", pairs[which][1]))
    back1 = home(merge(own1, *came))
    so_far = lax.optimization_barrier(widened + mix(0, back_own0))
    total = so_far + from_far.astype(F32) + from_near.astype(F32) + mix(1, back1)
    return (attended, total.astype(BF16))


def solution(mesh):
    placed = (
        P("ctx", "grp"),
        P("ctx", "grp"),
        P("ctx", "grp"),
        P("grp", "ctx"),
        P(("ctx", "grp"), None),
        P(),
        P(),
        P(("ctx", "grp"), None),
        P(("ctx", "grp"), None),
        P("ctx", None, "grp"),
        P("ctx", None, "grp"),
        P("ctx", "grp", None),
    )

    return jax.shard_map(
        on_device,
        mesh=mesh,
        in_specs=placed,
        out_specs=(P(("ctx", "grp"), None), P(("ctx", "grp"), None)),
        check_vma=False,
    )
```
